768 devices in a mesh: island: 16 (over x_hi, y), fsdp: 12 (over z), tensor: 4 (over x_lo, core).
Axes of the slice: x: 4 (x_hi: 2, x_lo: 2; x = x_hi * 2 + x_lo), y: 8, z: 12, core: 2. Of those that a mesh axis runs over, the one named last changes fastest.
Arguments:
- tokens: bfloat16 [24576, 6144], P(('island', 'fsdp')), may hold values from -6 to 6
- key_weight: bfloat16 [16, 6144, 1024], P('island', 'fsdp', 'tensor'), may hold values from -0.078125 to 0.078125
- key_cotangent: bfloat16 [24576, 1024], P(('island', 'fsdp'), 'tensor'), may hold values from -6 to 6
- local_frag: bfloat16 [16, 2, 6144, 2048], P('island', None, 'fsdp', 'tensor'), may hold values from -6 to 6
- outer_frag: float32 [2, 6144, 2048], P(None, 'fsdp', 'tensor'), may hold values from -6 to 6
- momentum: float32 [2, 6144, 2048], P(None, 'fsdp', 'tensor'), may hold values from -6 to 6
Outputs:
- keys: bfloat16 [24576, 1024], P(('island', 'fsdp'), 'tensor')
- input_grad: bfloat16 [24576, 6144], P(('island', 'fsdp', 'tensor'))
- weight_grad: bfloat16 [16, 6144, 1024], P('island', 'fsdp', 'tensor')
- new_outer: float32 [2, 6144, 2048], P(None, 'fsdp', 'tensor')
- new_momentum: float32 [2, 6144, 2048], P(None, 'fsdp', 'tensor')
The draws below stay inside these ranges and needn't reach their ends.
All inputs are finite; a program needn't handle non-finite values.
Results may differ from the reference program's by a relative error of at most 0.015.
Values may be sent and summed in bfloat16 or wider, within the bound.
A program may use at most 64 MiB of HBM per device.

```python
import jax
import jax.numpy as jnp
from jax import lax

D = 6144
KVW = 1024
FRAG_LAYERS = 2
TOK_DEV = 128
TOKENS = 24576
N_ISLAND = 16
N_FSDP = 12
N_TENSOR = 4


def shard_levels(stream_key, dims, cuts, low, top_value):
    def one(position, blocks):
        heights = jax.random.uniform(jax.random.fold_in(jax.random.fold_in(stream_key, 6), position), (blocks,), jnp.float32, low / len(cuts), top_value / len(cuts))
        return jnp.repeat(jnp.exp(heights), dims[position] // blocks).reshape((-1,) + (1,) * (len(dims) - position - 1))

    factor_of = one(*cuts[0])
    for cut in cuts[1:]:
        factor_of = factor_of * one(*cut)
    return factor_of


def normal_values(stream_key, dims, deviation, limit, split=(), kind=jnp.bfloat16):
    drawn = jax.random.normal(stream_key, dims, jnp.float32) * deviation
    if len(split) > 0:
        drawn = shard_levels(stream_key, dims, split, -0.22, 0.18) * drawn
    return jnp.clip(drawn, min=-limit, max=limit).astype(kind)


def setup_inputs(seed: int = 0) -> dict:
    seeds = jax.random.split(jax.random.key(seed), 7)
    tokens = normal_values(seeds[0], (TOKENS, D), 1.0, 6.0, ((0, 192),))
    key_weight = normal_values(seeds[1], (N_ISLAND, D, KVW), D ** -0.5, 0.078125, ((0, 16), (1, 12), (2, 4)))
    key_cotangent = normal_values(seeds[2], (TOKENS, KVW), 1.0, 6.0, ((0, 192), (1, 4)))
    local_frag = normal_values(seeds[3], (N_ISLAND, FRAG_LAYERS, D, 2 * KVW), 1.0, 6.0, ((0, 16), (2, 12), (3, 4)))
    outer_frag = normal_values(seeds[4], (FRAG_LAYERS, D, 2 * KVW), 1.0, 6.0, ((1, 12), (2, 4)), jnp.float32)
    momentum = normal_values(seeds[5], (FRAG_LAYERS, D, 2 * KVW), 1.0, 6.0, ((1, 12), (2, 4)), jnp.float32)
    return {"tokens": tokens, "key_weight": key_weight, "key_cotangent": key_cotangent, "local_frag": local_frag, "outer_frag": outer_frag, "momentum": momentum}


outer_rate = 0.7
beta_outer = 0.9


def island_work(bundle):
    tok_block, weight_block, cotangent_block = bundle
    keys = jnp.dot(tok_block, weight_block, preferred_element_type=jnp.float32).astype(jnp.bfloat16)
    head_cols = KVW // N_TENSOR
    input_sum = jnp.zeros((tok_block.shape[0], D), jnp.float32)
    for member in range(N_TENSOR):
        grad_part = jnp.dot(cotangent_block[:, member * head_cols:(member + 1) * head_cols],
                            weight_block[:, member * head_cols:(member + 1) * head_cols].T,
                            preferred_element_type=jnp.float32)
        input_sum = input_sum + grad_part.astype(jnp.bfloat16).astype(jnp.float32)
    weight_sum = jnp.zeros((D, KVW), jnp.float32)
    for member in range(N_FSDP):
        tok_rows = tok_block[member * TOK_DEV:(member + 1) * TOK_DEV]
        cot_rows = cotangent_block[member * TOK_DEV:(member + 1) * TOK_DEV]
        grad_part = jnp.dot(tok_rows.T, cot_rows, preferred_element_type=jnp.float32)
        weight_sum = weight_sum + grad_part.astype(jnp.bfloat16).astype(jnp.float32)
    return keys, input_sum.astype(jnp.bfloat16), weight_sum.astype(jnp.bfloat16)


def reference(tokens, key_weight, key_cotangent, local_frag, outer_frag, momentum):
    island_rows = TOK_DEV * N_FSDP
    tok_all = tokens.reshape(N_ISLAND, island_rows, D)
    cot_all = key_cotangent.reshape(N_ISLAND, island_rows, KVW)
    keys, input_grad, weight_grad = lax.map(island_work, (tok_all, key_weight, cot_all))
    frag_sum = jnp.zeros(outer_frag.shape, jnp.float32)
    for member in range(N_ISLAND):
        frag_sum = frag_sum + local_frag[member].astype(jnp.float32)
    average = outer_frag - frag_sum / N_ISLAND
    new_momentum = beta_outer * momentum + average
    new_outer = outer_frag - outer_rate * (average + beta_outer * new_momentum)
    return (keys.reshape(N_ISLAND * island_rows, KVW), input_grad.reshape(N_ISLAND * island_rows, D),
            weight_grad, new_outer, new_momentum)
```

```python
import jax
import jax.numpy as jnp
from jax import lax
from jax.experimental import pallas as pl
from jax.experimental.pallas import tpu as pltpu
from jax.sharding import PartitionSpec as P

outer_rate = 0.7
beta_outer = 0.9
MESH = pl.DeviceIdType.MESH
F, T, Y = 12, 4, 8
QR, DB, KT = 32, 512, 256
AGP, AGM = 6, 5
RSP, RSM = 5, 6
YP = (4, 3)
YM = (3, 4)
bf16, f32 = jnp.bfloat16, jnp.float32


def kernel(tok, w, cot, frag, outer, mom, keys_o, dx_o, dw_o, no_o, nm_o,
           xa, ca, wg, dxs, kp, ksp, ksm, krp, krm, kfin, dwp, dwr, dws, dwx, dwf,
           fr, yss, yrr, ys, xr, sm, ov, mv, nov, nmv,
           lsem, tks, tkr, cts, ctr, wss, wsr, ags, agr, dxsm, dxr, kss, ksr, kts, ktr,
           dwss, dwsr, yrs, yrrs, xss, xsr, yas, yar, osem):
    isl = lax.axis_index("island")
    f = lax.axis_index("fsdp")
    t = lax.axis_index("tensor")
    y = lax.rem(isl, Y)
    xh = isl - y
    fz = lambda k: lax.rem(f + (k + F), F)
    ty = lambda k: lax.rem(t + (k + T), T)
    yy = lambda k: lax.rem(y + (k + 2 * Y), Y)
    yd = lambda k: {"island": xh + yy(k)}
    xpart = {"island": lax.rem(isl + Y, 2 * Y)}
    core = lax.rem(t, 2)
    xlo = lax.div(t, 2)
    tc = t + 1 - 2 * core
    tx = ty(2)
    pending = []

    def local(src, dst, sem):
        c = pltpu.make_async_copy(src, dst, sem)
        c.start()
        return c

    def rc(src, dst, ss, rs, dev):
        return pltpu.make_async_remote_copy(src_ref=src, dst_ref=dst, send_sem=ss, recv_sem=rs,
                                            device_id=dev, device_id_type=MESH)

    def send(*a):
        c = rc(*a)
        c.start()
        pending.append(c)

    def got(dst, rs, ss, dev):
        rc(dst, dst, ss, rs, dev).wait_recv()

    cot_rows = lambda q: cot.at[pl.ds(pl.multiple_of(q * QR, QR), QR), :]
    tok_blk = lambda b: tok.at[pl.ds(pl.multiple_of(t * QR, QR), QR), pl.ds(pl.multiple_of(b * DB, DB), DB)]
    dx_blk = lambda b: dx_o.at[:, pl.ds(pl.multiple_of(b * DB, DB), DB)]

    bar = pltpu.get_barrier_semaphore()
    peers = [{"fsdp": fz(k)} for k in range(1, F)] + [{"tensor": ty(k)} for k in range(1, T)]
    peers += [yd(1), yd(-1), xpart]
    for d in peers:
        pl.semaphore_signal(bar, inc=1, device_id=d, device_id_type=MESH)

    l_w = local(w, wg.at[t], lsem.at[0])
    l_c = local(cot_rows(t), ca.at[f, t], lsem.at[1])
    l_x = local(tok_blk(f), xa.at[f], lsem.at[2])
    l_f = local(frag, fr, lsem.at[3])
    pl.semaphore_wait(bar, len(peers))

    for j in range(1, T):
        send(cot_rows(ty(j)), ca.at[f, t], cts.at[j - 1], ctr.at[j - 1], {"tensor": ty(j)})
    for h in range(2):
        send(frag.at[yy(YP[h]), h], yrr.at[0, h, 0], yrs.at[0, h, 0], yrrs.at[0, h, 0], yd(1))
        send(frag.at[yy(-YM[h]), h], yrr.at[1, h, 0], yrs.at[1, h, 0], yrrs.at[1, h, 0], yd(-1))
    send(w, wg.at[t], wss.at[0], wsr.at[0], {"tensor": tx})
    send(w, wg.at[t], wss.at[1], wsr.at[1], {"tensor": tc})
    for k in (6, 5, -5, 4, -4, 3, -3, 2, -2, 1, -1):
        b = fz(k)
        i = k % F - 1
        send(tok_blk(b), xa.at[f], tks.at[i], tkr.at[i], {"fsdp": b})
    l_o = local(outer, ov, lsem.at[4])
    l_m = local(mom, mv, lsem.at[5])

    l_c.wait()
    for j in range(1, T):
        got(ca.at[f, ty(-j)], ctr.at[j - 1], cts.at[j - 1], {"tensor": ty(-j)})

    def ag_send(s):
        if s < AGP:
            b = fz(-s)
            send(ca.at[b], ca.at[b], ags.at[0, s], agr.at[0, s], {"fsdp": fz(1)})
        if s < AGM:
            b = fz(s)
            send(ca.at[b], ca.at[b], ags.at[1, s], agr.at[1, s], {"fsdp": fz(-1)})

    def ag_step(s):
        if s <= AGP:
            got(ca.at[fz(-s)], agr.at[0, s - 1], ags.at[0, s - 1], {"fsdp": fz(-1)})
        if s <= AGM:
            got(ca.at[fz(s)], agr.at[1, s - 1], ags.at[1, s - 1], {"fsdp": fz(1)})
        ag_send(s)

    def dx_step(s):
        ks = [k for k, ok in ((-s, s <= AGP), (s, s <= AGM and s > 0)) if ok]
        bs = [fz(k) for k in ks]
        acc = None
        for q in range(T):
            lhs = jnp.concatenate([ca[b, q] for b in bs], axis=0) if len(bs) > 1 else ca[bs[0], q]
            p = lax.dot_general(lhs, wg[q], (((1,), (1,)), ((), ())), preferred_element_type=f32)
            acc = p if acc is None else acc + p
        for n, (k, b) in enumerate(zip(ks, bs)):
            dxs[b] = acc[n * QR:(n + 1) * QR].astype(bf16)
            if k != 0:
                i = k % F - 1
                send(dxs.at[b], dx_blk(f), dxsm.at[i], dxr.at[i], {"fsdp": b})
        if s == 0:
            pending_local.append(local(dxs.at[f], dx_blk(f), osem.at[0]))

    pending_local = []

    def y_step(s):
        for h in range(2):
            for d, hops, sgn in ((0, YP[h], 1), (1, YM[h], -1)):
                if s < hops:
                    got(yrr.at[d, h, s - 1], yrrs.at[d, h, s - 1], yrs.at[d, h, s - 1], yd(-sgn))
                    b = yy(sgn * (hops - s))
                    yss[d, h, s - 1] = (yrr[d, h, s - 1].astype(f32) + fr[b, h].astype(f32)).astype(bf16)
                    send(yss.at[d, h, s - 1], yrr.at[d, h, s], yrs.at[d, h, s], yrrs.at[d, h, s], yd(sgn))

    def y_last():
        for h in range(2):
            got(yrr.at[0, h, YP[h] - 1], yrrs.at[0, h, YP[h] - 1], yrs.at[0, h, YP[h] - 1], yd(-1))
            got(yrr.at[1, h, YM[h] - 1], yrrs.at[1, h, YM[h] - 1], yrs.at[1, h, YM[h] - 1], yd(1))
            ys[h] = (yrr[0, h, YP[h] - 1].astype(f32) + yrr[1, h, YM[h] - 1].astype(f32)
                     + fr[y, h].astype(f32)).astype(bf16)
            send(ys.at[h], xr.at[h], xss.at[h], xsr.at[h], xpart)

    def update(b, h):
        avg = ov[b, h] - sm[b, h].astype(f32) * (1.0 / (2 * Y))
        nm = beta_outer * mv[b, h] + avg
        nmv[b, h] = nm
        nov[b, h] = ov[b, h] - outer_rate * (avg + beta_outer * nm)

    def ya_send(s):
        for h in range(2):
            if s < YP[h]:
                b = yy(-s)
                send(sm.at[b, h], sm.at[b, h], yas.at[0, h, s], yar.at[0, h, s], yd(1))
            if s < YM[h]:
                b = yy(s)
                send(sm.at[b, h], sm.at[b, h], yas.at[1, h, s], yar.at[1, h, s], yd(-1))

    def ya_first():
        for h in range(2):
            got(xr.at[h], xsr.at[h], xss.at[h], xpart)
            sm[y, h] = (ys[h].astype(f32) + xr[h].astype(f32)).astype(bf16)
        ya_send(0)

    def ya_step(s):
        done = []
        for h in range(2):
            if s <= YP[h]:
                b = yy(-s)
                got(sm.at[b, h], yar.at[0, h, s - 1], yas.at[0, h, s - 1], yd(-1))
                done.append((b, h))
            if s <= YM[h]:
                b = yy(s)
                got(sm.at[b, h], yar.at[1, h, s - 1], yas.at[1, h, s - 1], yd(1))
                done.append((b, h))
        ya_send(s)
        for b, h in done:
            update(b, h)

    def k_all():
        l_x.wait()
        for k in range(1, F):
            got(xa.at[fz(-k)], tkr.at[k - 1], tks.at[k - 1], {"fsdp": fz(-k)})

        def one(q, c):
            r = jnp.dot(xa[...].reshape(F * QR, DB), wg[q], preferred_element_type=f32)
            kp[q] = r.reshape(F, QR, KT)
            return c
        lax.fori_loop(0, T, one, 0)

    def k_step(s):
        for d, hops, sgn, rv, sd in ((0, RSP, 1, krp, ksp), (1, RSM, -1, krm, ksm)):
            if s < hops:
                b = fz(sgn * (hops - s))
                v = kp[:, b]
                if s > 0:
                    got(rv.at[s - 1], ksr.at[d, s - 1], kss.at[d, s - 1], {"fsdp": fz(-sgn)})
                    v = v + rv[s - 1].astype(f32)
                sd[s] = v.astype(bf16)
                send(sd.at[s], rv.at[s], kss.at[d, s], ksr.at[d, s], {"fsdp": fz(sgn)})

    def k_last():
        got(krp.at[RSP - 1], ksr.at[0, RSP - 1], kss.at[0, RSP - 1], {"fsdp": fz(-1)})
        got(krm.at[RSM - 1], ksr.at[1, RSM - 1], kss.at[1, RSM - 1], {"fsdp": fz(1)})
        kfin[...] = (kp[:, f] + krp[RSP - 1].astype(f32) + krm[RSM - 1].astype(f32)).astype(bf16)
        mine = keys_o.at[pl.ds(pl.multiple_of(t * QR, QR), QR), :]
        for j in range(1, T):
            q = ty(j)
            send(kfin.at[q], mine, kts.at[j - 1], ktr.at[j - 1], {"tensor": q})
        pending_local.append(local(kfin.at[t], mine, osem.at[1]))

    def w_all():
        def one(q, c):
            r = lax.dot_general(xa[...].reshape(F * QR, DB), ca[:, q].reshape(F * QR, KT),
                                (((0,), (0,)), ((), ())), preferred_element_type=f32)
            dwp[q] = r.astype(bf16)
            return c
        lax.fori_loop(0, T, one, 0)
        for m in range(2):
            send(dwp.at[2 * m + 1 - core], dwr.at[m], dwss.at[m], dwsr.at[m], {"tensor": tc})

    def w_mid():
        for m in range(2):
            got(dwr.at[m], dwsr.at[m], dwss.at[m], {"tensor": tc})
        o = 1 - xlo
        dws[...] = (dwp[2 * o + core].astype(f32) + dwr[o].astype(f32)).astype(bf16)
        send(dws, dwx, dwss.at[2], dwsr.at[2], {"tensor": tx})

    def w_last():
        got(dwx, dwsr.at[2], dwss.at[2], {"tensor": tx})
        dwf[...] = (dwp[2 * xlo + core].astype(f32) + dwr[xlo].astype(f32) + dwx[...].astype(f32)).astype(bf16)
        pending_local.append(local(dwf, dw_o, osem.at[2]))

    ag_send(0)
    l_f.wait()
    y_step(1)
    ag_step(1)
    got(wg.at[tx], wsr.at[0], wss.at[0], {"tensor": tx})
    send(wg.at[tx], wg.at[tx], wss.at[2], wsr.at[2], {"tensor": tc})
    y_step(2)
    ag_step(2)
    l_w.wait()
    got(wg.at[tc], wsr.at[1], wss.at[1], {"tensor": tc})
    txc = lax.rem(tc + 2, T)
    got(wg.at[txc], wsr.at[2], wss.at[2], {"tensor": tc})
    dx_step(2)
    dx_step(1)
    y_step(3)
    ag_step(3)
    dx_step(3)
    dx_step(0)
    y_last()
    ag_step(4)
    dx_step(4)
    ya_first()
    k_all()
    k_step(0)
    ag_step(5)
    dx_step(5)
    k_step(1)
    l_o.wait()
    l_m.wait()
    ya_step(1)
    update(y, 0)
    update(y, 1)
    ag_step(6)
    dx_step(6)
    k_step(2)
    ya_step(2)
    w_all()
    k_step(3)
    ya_step(3)
    w_mid()
    k_step(4)
    ya_step(4)
    pending_local.append(local(nov, no_o, osem.at[3]))
    pending_local.append(local(nmv, nm_o, osem.at[4]))
    k_step(5)
    w_last()
    k_last()
    for k in range(1, F):
        got(dx_blk(fz(-k)), dxr.at[k - 1], dxsm.at[k - 1], {"fsdp": fz(-k)})
    for j in range(1, T):
        q = ty(-j)
        got(keys_o.at[pl.ds(pl.multiple_of(q * QR, QR), QR), :], ktr.at[j - 1], kts.at[j - 1], {"tensor": q})
    for c in pending_local:
        c.wait()
    for c in pending:
        c.wait_send()


def body(tokens, key_weight, key_cotangent, local_frag, outer_frag, momentum):
    FS = (Y, 2, 64, 512)
    V, DMA = pltpu.VMEM, pltpu.SemaphoreType.DMA
    blk = (T, QR, KT)
    any_ = pl.BlockSpec(memory_space=pl.ANY)
    keys, dx, dw, no, nm = pl.pallas_call(
        kernel,
        out_shape=(
            jax.ShapeDtypeStruct((T * QR, KT), bf16),
            jax.ShapeDtypeStruct((QR, F * DB), bf16),
            jax.ShapeDtypeStruct((DB, KT), bf16),
            jax.ShapeDtypeStruct(FS, f32),
            jax.ShapeDtypeStruct(FS, f32),
        ),
        in_specs=[any_] * 6,
        out_specs=(any_,) * 5,
        scratch_shapes=[
            V((F, QR, DB), bf16), V((F,) + blk, bf16), V((T, DB, KT), bf16), V((F, QR, DB), bf16),
            V((T, F, QR, KT), f32), V((RSP,) + blk, bf16), V((RSM,) + blk, bf16),
            V((RSP,) + blk, bf16), V((RSM,) + blk, bf16), V(blk, bf16),
            V((T, DB, KT), bf16), V((2, DB, KT), bf16), V((DB, KT), bf16), V((DB, KT), bf16), V((DB, KT), bf16),
            V(FS, bf16), V((2, 2, 3, 64, 512), bf16), V((2, 2, 4, 64, 512), bf16),
            V((2, 64, 512), bf16), V((2, 64, 512), bf16), V(FS, bf16),
            V(FS, f32), V(FS, f32), V(FS, f32), V(FS, f32),
            DMA((6,)), DMA((11,)), DMA((11,)), DMA((3,)), DMA((3,)), DMA((3,)), DMA((3,)),
            DMA((2, 6)), DMA((2, 6)), DMA((11,)), DMA((11,)), DMA((2, 6)), DMA((2, 6)), DMA((3,)), DMA((3,)),
            DMA((3,)), DMA((3,)), DMA((2, 2, 4)), DMA((2, 2, 4)), DMA((2,)), DMA((2,)),
            DMA((2, 2, 4)), DMA((2, 2, 4)), DMA((5,)),
        ],
        compiler_params=pltpu.CompilerParams(collective_id=0, has_side_effects=True,
                                             vmem_limit_bytes=48 << 20),
    )(tokens, key_weight[0], key_cotangent, local_frag.reshape(FS), outer_frag.reshape(FS), momentum.reshape(FS))
    return keys, dx, dw[None], no.reshape(outer_frag.shape), nm.reshape(momentum.shape)


def solution(mesh):
    return jax.shard_map(
        body,
        mesh=mesh,
        in_specs=(
            P(("island", "fsdp"), None),
            P("island", "fsdp", "tensor"),
            P(("island", "fsdp"), "tensor"),
            P("island", None, "fsdp", "tensor"),
            P(None, "fsdp", "tensor"),
            P(None, "fsdp", "tensor"),
        ),
        out_specs=(
            P(("island", "fsdp"), "tensor"),
            P(("island", "fsdp", "tensor"), None),
            P("island", "fsdp", "tensor"),
            P(None, "fsdp", "tensor"),
            P(None, "fsdp", "tensor"),
        ),
        check_vma=False,
    )
```

```python
import jax
import jax.numpy as jnp
from jax import lax
from jax.experimental import pallas as pl
from jax.experimental.pallas import tpu as pltpu
from jax.sharding import PartitionSpec as P

outer_rate = 0.7
beta_outer = 0.9
MESH = pl.DeviceIdType.MESH
F, T, Y = 12, 4, 8
QR, DB, KT = 32, 512, 256
AGP, AGM = 6, 5
RSP, RSM = 5, 6
YP = (4, 3)
YM = (3, 4)
bf16, f32 = jnp.bfloat16, jnp.float32


def kernel(tok, w, cot, frag, outer, mom, keys_o, dx_o, dw_o, no_o, nm_o,
           xa, ca, wg, dxs, kp, ksp, ksm, krp, krm, kfin, dwp, dwr, dws, dwx,
           fr, yss, yrr, ys, xr, sm, ov, mv,
           lsem, tks, tkr, cts, ctr, wss, wsr, ags, agr, dxsm, dxr, kss, ksr, kts, ktr,
           dwss, dwsr, yrs, yrrs, xss, xsr, yas, yar):
    isl = lax.axis_index("island")
    f = lax.axis_index("fsdp")
    t = lax.axis_index("tensor")
    y = lax.rem(isl, Y)
    xh = isl - y
    fz = lambda k: lax.rem(f + (k + F), F)
    ty = lambda k: lax.rem(t + (k + T), T)
    yy = lambda k: lax.rem(y + (k + 2 * Y), Y)
    yd = lambda k: {"island": xh + yy(k)}
    xpart = {"island": lax.rem(isl + Y, 2 * Y)}
    core = lax.rem(t, 2)
    xlo = lax.div(t, 2)
    tc = t + 1 - 2 * core
    tx = ty(2)
    pending = []

    def local(src, dst, sem):
        c = pltpu.make_async_copy(src, dst, sem)
        c.start()
        return c

    def rc(src, dst, ss, rs, dev):
        return pltpu.make_async_remote_copy(src_ref=src, dst_ref=dst, send_sem=ss, recv_sem=rs,
                                            device_id=dev, device_id_type=MESH)

    def send(*a):
        c = rc(*a)
        c.start()
        pending.append(c)

    def got(dst, rs, ss, dev):
        rc(dst, dst, ss, rs, dev).wait_recv()

    cot_rows = lambda q: cot.at[pl.ds(pl.multiple_of(q * QR, QR), QR), :]
    tok_blk = lambda b: tok.at[pl.ds(pl.multiple_of(t * QR, QR), QR), pl.ds(pl.multiple_of(b * DB, DB), DB)]
    dx_blk = lambda b: dx_o.at[:, pl.ds(pl.multiple_of(b * DB, DB), DB)]

    bar = pltpu.get_barrier_semaphore()
    peers = [{"fsdp": fz(k)} for k in range(1, F)] + [{"tensor": ty(k)} for k in range(1, T)]
    peers += [yd(1), yd(-1), xpart]
    for d in peers:
        pl.semaphore_signal(bar, inc=1, device_id=d, device_id_type=MESH)

    l_w = local(w, wg.at[t], lsem.at[0])
    l_c = local(cot_rows(t), ca.at[f, t], lsem.at[1])
    l_x = local(tok_blk(f), xa.at[f], lsem.at[2])
    l_f = local(frag, fr, lsem.at[3])
    pl.semaphore_wait(bar, len(peers))

    for j in range(1, T):
        send(cot_rows(ty(j)), ca.at[f, t], cts.at[j - 1], ctr.at[j - 1], {"tensor": ty(j)})
    for h in range(2):
        send(frag.at[yy(YP[h]), h], yrr.at[0, h, 0], yrs.at[0, h, 0], yrrs.at[0, h, 0], yd(1))
        send(frag.at[yy(-YM[h]), h], yrr.at[1, h, 0], yrs.at[1, h, 0], yrrs.at[1, h, 0], yd(-1))
    send(w, wg.at[t], wss.at[0], wsr.at[0], {"tensor": tx})
    send(w, wg.at[t], wss.at[1], wsr.at[1], {"tensor": tc})
    def tok_send(ks):
        for k in ks:
            b = fz(k)
            i = k % F - 1
            send(tok_blk(b), xa.at[f], tks.at[i], tkr.at[i], {"fsdp": b})

    tok_send((6, 5, -5))
    l_o = local(outer, ov, lsem.at[4])
    l_m = local(mom, mv, lsem.at[5])

    l_c.wait()
    for j in range(1, T):
        got(ca.at[f, ty(-j)], ctr.at[j - 1], cts.at[j - 1], {"tensor": ty(-j)})

    def ag_send(s):
        if s < AGP:
            b = fz(-s)
            send(ca.at[b], ca.at[b], ags.at[0, s], agr.at[0, s], {"fsdp": fz(1)})
        if s < AGM:
            b = fz(s)
            send(ca.at[b], ca.at[b], ags.at[1, s], agr.at[1, s], {"fsdp": fz(-1)})

    def ag_step(s):
        if s <= AGP:
            got(ca.at[fz(-s)], agr.at[0, s - 1], ags.at[0, s - 1], {"fsdp": fz(-1)})
        if s <= AGM:
            got(ca.at[fz(s)], agr.at[1, s - 1], ags.at[1, s - 1], {"fsdp": fz(1)})
        ag_send(s)

    def dx_step(s):
        ks = [k for k, ok in ((-s, s <= AGP), (s, s <= AGM and s > 0)) if ok]
        bs = [fz(k) for k in ks]
        acc = None
        for q in range(T):
            lhs = jnp.concatenate([ca[b, q] for b in bs], axis=0) if len(bs) > 1 else ca[bs[0], q]
            p = lax.dot_general(lhs, wg[q], (((1,), (1,)), ((), ())), preferred_element_type=f32)
            acc = p if acc is None else acc + p
        for n, (k, b) in enumerate(zip(ks, bs)):
            r = acc[n * QR:(n + 1) * QR].astype(bf16)
            if k == 0:
                dx_o[:, pl.ds(pl.multiple_of(f * DB, DB), DB)] = r
            else:
                i = k % F - 1
                dxs[b] = r
                send(dxs.at[b], dx_blk(f), dxsm.at[i], dxr.at[i], {"fsdp": b})

    def y_step(s):
        for h in range(2):
            for d, hops, sgn in ((0, YP[h], 1), (1, YM[h], -1)):
                if s < hops:
                    got(yrr.at[d, h, s - 1], yrrs.at[d, h, s - 1], yrs.at[d, h, s - 1], yd(-sgn))
                    b = yy(sgn * (hops - s))
                    yss[d, h, s - 1] = (yrr[d, h, s - 1].astype(f32) + fr[b, h].astype(f32)).astype(bf16)
                    send(yss.at[d, h, s - 1], yrr.at[d, h, s], yrs.at[d, h, s], yrrs.at[d, h, s], yd(sgn))

    def y_last():
        for h in range(2):
            got(yrr.at[0, h, YP[h] - 1], yrrs.at[0, h, YP[h] - 1], yrs.at[0, h, YP[h] - 1], yd(-1))
            got(yrr.at[1, h, YM[h] - 1], yrrs.at[1, h, YM[h] - 1], yrs.at[1, h, YM[h] - 1], yd(1))
            ys[h] = (yrr[0, h, YP[h] - 1].astype(f32) + yrr[1, h, YM[h] - 1].astype(f32)
                     + fr[y, h].astype(f32)).astype(bf16)
            send(ys.at[h], xr.at[h], xss.at[h], xsr.at[h], xpart)

    def update(b, h):
        avg = ov[b, h] - sm[b, h].astype(f32) * (1.0 / (2 * Y))
        nm = beta_outer * mv[b, h] + avg
        nm_o[b, h] = nm
        no_o[b, h] = ov[b, h] - outer_rate * (avg + beta_outer * nm)

    def ya_send(s):
        for h in range(2):
            if s < YP[h]:
                b = yy(-s)
                send(sm.at[b, h], sm.at[b, h], yas.at[0, h, s], yar.at[0, h, s], yd(1))
            if s < YM[h]:
                b = yy(s)
                send(sm.at[b, h], sm.at[b, h], yas.at[1, h, s], yar.at[1, h, s], yd(-1))

    def ya_first():
        for h in range(2):
            got(xr.at[h], xsr.at[h], xss.at[h], xpart)
            sm[y, h] = (ys[h].astype(f32) + xr[h].astype(f32)).astype(bf16)
        ya_send(0)

    def upd(s):
        for h in range(2):
            if s <= YP[h]:
                update(yy(-s), h)
            if 0 < s <= YM[h]:
                update(yy(s), h)

    def ya_step(s):
        for h in range(2):
            if s <= YP[h]:
                b = yy(-s)
                got(sm.at[b, h], yar.at[0, h, s - 1], yas.at[0, h, s - 1], yd(-1))
            if s <= YM[h]:
                b = yy(s)
                got(sm.at[b, h], yar.at[1, h, s - 1], yas.at[1, h, s - 1], yd(1))
        ya_send(s)

    def k_make(s):
        ks = [k for k, ok in ((RSP - s, s <= RSP), (s - RSM, s < RSM)) if ok]
        for k in ks:
            if k == 0:
                l_x.wait()
            else:
                i = (-k) % F - 1
                got(xa.at[fz(k)], tkr.at[i], tks.at[i], {"fsdp": fz(k)})
        bs = [fz(k) for k in ks]
        lhs = jnp.concatenate([xa[b] for b in bs], axis=0) if len(bs) > 1 else xa[bs[0]]
        for q in range(T):
            r = jnp.dot(lhs, wg[q], preferred_element_type=f32)
            for n, b in enumerate(bs):
                kp[q, b] = r[n * QR:(n + 1) * QR]

    def k_step(s):
        for d, hops, sgn, rv, sd in ((0, RSP, 1, krp, ksp), (1, RSM, -1, krm, ksm)):
            if s < hops:
                b = fz(sgn * (hops - s))
                v = kp[:, b]
                if s > 0:
                    got(rv.at[s - 1], ksr.at[d, s - 1], kss.at[d, s - 1], {"fsdp": fz(-sgn)})
                    v = v + rv[s - 1].astype(f32)
                sd[s] = v.astype(bf16)
                send(sd.at[s], rv.at[s], kss.at[d, s], ksr.at[d, s], {"fsdp": fz(sgn)})

    def k_last():
        got(krp.at[RSP - 1], ksr.at[0, RSP - 1], kss.at[0, RSP - 1], {"fsdp": fz(-1)})
        got(krm.at[RSM - 1], ksr.at[1, RSM - 1], kss.at[1, RSM - 1], {"fsdp": fz(1)})
        kfin[...] = (kp[:, f] + krp[RSP - 1].astype(f32) + krm[RSM - 1].astype(f32)).astype(bf16)
        rows = pl.ds(pl.multiple_of(t * QR, QR), QR)
        mine = keys_o.at[rows, :]
        for j in range(1, T):
            q = ty(j)
            send(kfin.at[q], mine, kts.at[j - 1], ktr.at[j - 1], {"tensor": q})
        keys_o[rows, :] = kfin[t]

    def w_all():
        def one(q, c):
            r = lax.dot_general(xa[...].reshape(F * QR, DB), ca[:, q].reshape(F * QR, KT),
                                (((0,), (0,)), ((), ())), preferred_element_type=f32)
            dwp[q] = r.astype(bf16)
            return c
        lax.fori_loop(0, T, one, 0)
        for m in range(2):
            send(dwp.at[2 * m + 1 - core], dwr.at[m], dwss.at[m], dwsr.at[m], {"tensor": tc})

    def w_mid():
        for m in range(2):
            got(dwr.at[m], dwsr.at[m], dwss.at[m], {"tensor": tc})
        o = 1 - xlo
        dws[...] = (dwp[2 * o + core].astype(f32) + dwr[o].astype(f32)).astype(bf16)
        send(dws, dwx, dwss.at[2], dwsr.at[2], {"tensor": tx})

    def w_last():
        got(dwx, dwsr.at[2], dwss.at[2], {"tensor": tx})
        dw_o[...] = (dwp[2 * xlo + core].astype(f32) + dwr[xlo].astype(f32) + dwx[...].astype(f32)).astype(bf16)

    ag_send(0)
    tok_send((4, -4, 3, -3))
    l_f.wait()
    y_step(1)
    ag_step(1)
    tok_send((2, -2, 1, -1))
    y_step(2)
    ag_step(2)
    got(wg.at[tx], wsr.at[0], wss.at[0], {"tensor": tx})
    send(wg.at[tx], wg.at[tx], wss.at[2], wsr.at[2], {"tensor": tc})
    l_w.wait()
    got(wg.at[tc], wsr.at[1], wss.at[1], {"tensor": tc})
    txc = lax.rem(tc + 2, T)
    got(wg.at[txc], wsr.at[2], wss.at[2], {"tensor": tc})
    k_make(0)
    k_step(0)
    dx_step(1)
    y_step(3)
    ag_step(3)
    k_make(1)
    k_step(1)
    dx_step(2)
    y_last()
    ag_step(4)
    k_make(2)
    k_step(2)
    dx_step(3)
    ya_first()
    ag_step(5)
    k_make(3)
    k_step(3)
    dx_step(4)
    ya_step(1)
    ag_step(6)
    dx_step(6)
    k_make(4)
    k_step(4)
    dx_step(5)
    k_make(5)
    k_step(5)
    w_all()
    ya_step(2)
    dx_step(0)
    w_mid()
    ya_step(3)
    k_last()
    l_o.wait()
    l_m.wait()
    for s in range(4):
        upd(s)
    ya_step(4)
    upd(4)
    w_last()
    for k in range(1, F):
        got(dx_blk(fz(-k)), dxr.at[k - 1], dxsm.at[k - 1], {"fsdp": fz(-k)})
    for j in range(1, T):
        q = ty(-j)
        got(keys_o.at[pl.ds(pl.multiple_of(q * QR, QR), QR), :], ktr.at[j - 1], kts.at[j - 1], {"tensor": q})
    for c in pending:
        c.wait_send()


def flush(*refs):
    n = len(refs) // 2
    sem = refs[-1]
    copies = [pltpu.make_async_copy(refs[i], refs[n + i], sem.at[i]) for i in (3, 4, 1, 2, 0)]
    for c in copies:
        c.start()
    for c in copies:
        c.wait()


def body(tokens, key_weight, key_cotangent, local_frag, outer_frag, momentum):
    FS = (Y, 2, 64, 512)
    V, DMA = pltpu.VMEM, pltpu.SemaphoreType.DMA
    blk = (T, QR, KT)
    hbm = pl.BlockSpec(memory_space=pltpu.HBM)
    vmem = pl.BlockSpec(memory_space=pltpu.VMEM)
    outs = (
        jax.ShapeDtypeStruct((T * QR, KT), bf16),
        jax.ShapeDtypeStruct((QR, F * DB), bf16),
        jax.ShapeDtypeStruct((DB, KT), bf16),
        jax.ShapeDtypeStruct(FS, f32),
        jax.ShapeDtypeStruct(FS, f32),
    )
    fixed = lambda a: pltpu.with_memory_space_constraint(a, pltpu.HBM)
    made = pl.pallas_call(
        kernel,
        out_shape=tuple(V(o.shape, o.dtype) for o in outs),
        in_specs=[hbm] * 6,
        out_specs=(vmem,) * 5,
        scratch_shapes=[
            V((F, QR, DB), bf16), V((F,) + blk, bf16), V((T, DB, KT), bf16), V((F, QR, DB), bf16),
            V((T, F, QR, KT), f32), V((RSP,) + blk, bf16), V((RSM,) + blk, bf16),
            V((RSP,) + blk, bf16), V((RSM,) + blk, bf16), V(blk, bf16),
            V((T, DB, KT), bf16), V((2, DB, KT), bf16), V((DB, KT), bf16), V((DB, KT), bf16),
            V(FS, bf16), V((2, 2, 3, 64, 512), bf16), V((2, 2, 4, 64, 512), bf16),
            V((2, 64, 512), bf16), V((2, 64, 512), bf16), V(FS, bf16),
            V(FS, f32), V(FS, f32),
            DMA((6,)), DMA((11,)), DMA((11,)), DMA((3,)), DMA((3,)), DMA((3,)), DMA((3,)),
            DMA((2, 6)), DMA((2, 6)), DMA((11,)), DMA((11,)), DMA((2, 6)), DMA((2, 6)), DMA((3,)), DMA((3,)),
            DMA((3,)), DMA((3,)), DMA((2, 2, 4)), DMA((2, 2, 4)), DMA((2,)), DMA((2,)),
            DMA((2, 2, 4)), DMA((2, 2, 4)),
        ],
        compiler_params=pltpu.CompilerParams(collective_id=0, has_side_effects=True,
                                             vmem_limit_bytes=40 << 20),
    )(*map(fixed, (tokens, key_weight[0], key_cotangent, local_frag.reshape(FS), outer_frag.reshape(FS), momentum.reshape(FS))))
    keys, dx, dw, no, nm = pl.pallas_call(
        flush,
        out_shape=outs,
        in_specs=[vmem] * 5,
        out_specs=(hbm,) * 5,
        scratch_shapes=[DMA((5,))],
        compiler_params=pltpu.CompilerParams(vmem_limit_bytes=1 << 20),
    )(*made)
    return keys, dx, dw[None], no.reshape(outer_frag.shape), nm.reshape(momentum.shape)


def solution(mesh):
    return jax.shard_map(
        body,
        mesh=mesh,
        in_specs=(
            P(("island", "fsdp"), None),
            P("island", "fsdp", "tensor"),
            P(("island", "fsdp"), "tensor"),
            P("island", None, "fsdp", "tensor"),
            P(None, "fsdp", "tensor"),
            P(None, "fsdp", "tensor"),
        ),
        out_specs=(
            P(("island", "fsdp"), "tensor"),
            P(("island", "fsdp", "tensor"), None),
            P("island", "fsdp", "tensor"),
            P(None, "fsdp", "tensor"),
            P(None, "fsdp", "tensor"),
        ),
        check_vma=False,
    )
```

```python
import jax
import jax.numpy as jnp
from jax import lax
from jax.experimental import pallas as pl
from jax.experimental.pallas import tpu as pltpu
from jax.sharding import PartitionSpec as P

outer_rate = 0.7
beta_outer = 0.9
MESH = pl.DeviceIdType.MESH
F, T, Y = 12, 4, 8
QR, DB, KT = 32, 512, 256
AGP, AGM = 6, 5
RSP, RSM = 5, 6
YP = (4, 3)
YM = (3, 4)
bf16, f32 = jnp.bfloat16, jnp.float32


def kernel(tok, w, cot, frag, outer, mom, keys_o, dx_o, dw_o, no_o, nm_o,
           xa, ca, wg, dxs, kp, ksp, ksm, krp, krm, kfin, dwp, dwr, dws, dwx,
           fr, yss, yrr, ys, xr, sm, ov, mv,
           lsem, tks, tkr, cts, ctr, wss, wsr, ags, agr, dxsm, dxr, kss, ksr, kts, ktr,
           dwss, dwsr, yrs, yrrs, xss, xsr, yas, yar, wv):
    isl = lax.axis_index("island")
    f = lax.axis_index("fsdp")
    t = lax.axis_index("tensor")
    y = lax.rem(isl, Y)
    xh = isl - y
    fz = lambda k: lax.rem(f + (k + F), F)
    ty = lambda k: lax.rem(t + (k + T), T)
    yy = lambda k: lax.rem(y + (k + 2 * Y), Y)
    yd = lambda k: {"island": xh + yy(k)}
    xpart = {"island": lax.rem(isl + Y, 2 * Y)}
    core = lax.rem(t, 2)
    xlo = lax.div(t, 2)
    tc = t + 1 - 2 * core
    tx = ty(2)
    pending = []

    def local(src, dst, sem):
        c = pltpu.make_async_copy(src, dst, sem)
        c.start()
        return c

    def rc(src, dst, ss, rs, dev):
        return pltpu.make_async_remote_copy(src_ref=src, dst_ref=dst, send_sem=ss, recv_sem=rs,
                                            device_id=dev, device_id_type=MESH)

    def send(*a):
        c = rc(*a)
        c.start()
        pending.append(c)

    def got(dst, rs, ss, dev):
        rc(dst, dst, ss, rs, dev).wait_recv()

    cot_rows = lambda q: cot.at[pl.ds(pl.multiple_of(q * QR, QR), QR), :]
    tok_blk = lambda b: tok.at[pl.ds(pl.multiple_of(t * QR, QR), QR), pl.ds(pl.multiple_of(b * DB, DB), DB)]
    dx_blk = lambda b: dx_o.at[:, pl.ds(pl.multiple_of(b * DB, DB), DB)]

    bar = pltpu.get_barrier_semaphore()
    peers = [{"fsdp": fz(1)}, {"fsdp": fz(-1)}] + [{"tensor": ty(k)} for k in range(1, T)]
    peers += [yd(1), yd(-1), xpart]
    for d in peers:
        pl.semaphore_signal(bar, inc=1, device_id=d, device_id_type=MESH)

    l_w = local(w, wg.at[t], lsem.at[0])
    l_c = local(cot_rows(t), ca.at[f, t], lsem.at[1])
    l_x = local(tok_blk(f), xa.at[f], lsem.at[2])
    l_f = local(frag, fr, lsem.at[3])
    pl.semaphore_wait(bar, len(peers))

    for j in range(1, T):
        send(cot_rows(ty(j)), ca.at[f, t], cts.at[j - 1], ctr.at[j - 1], {"tensor": ty(j)})
    for h in range(2):
        send(frag.at[yy(YP[h]), h], yrr.at[0, h, 0], yrs.at[0, h, 0], yrrs.at[0, h, 0], yd(1))
        send(frag.at[yy(-YM[h]), h], yrr.at[1, h, 0], yrs.at[1, h, 0], yrrs.at[1, h, 0], yd(-1))
    send(w, wg.at[t], wss.at[0], wsr.at[0], {"tensor": tx})
    send(w, wg.at[t], wss.at[1], wsr.at[1], {"tensor": tc})
    def tok_send(ks):
        for k in ks:
            b = fz(k)
            i = k % F - 1
            send(tok_blk(b), xa.at[f], tks.at[i], tkr.at[i], {"fsdp": b})

    def wave():
        for n in range(F // 2):
            for d, sgn in ((0, 1), (1, -1)):
                if n > 0:
                    pl.semaphore_wait(wv.at[d, n - 1], 1)
                if n < F // 2 - 1:
                    pl.semaphore_signal(wv.at[d, n], inc=1, device_id={"fsdp": fz(sgn)}, device_id_type=MESH)

    tok_send((1, -1))
    l_o = local(outer, ov, lsem.at[4])
    l_m = local(mom, mv, lsem.at[5])

    l_c.wait()
    for j in range(1, T):
        got(ca.at[f, ty(-j)], ctr.at[j - 1], cts.at[j - 1], {"tensor": ty(-j)})

    def ag_send(s):
        if s < AGP:
            b = fz(-s)
            send(ca.at[b], ca.at[b], ags.at[0, s], agr.at[0, s], {"fsdp": fz(1)})
        if s < AGM:
            b = fz(s)
            send(ca.at[b], ca.at[b], ags.at[1, s], agr.at[1, s], {"fsdp": fz(-1)})

    def ag_step(s):
        if s <= AGP:
            got(ca.at[fz(-s)], agr.at[0, s - 1], ags.at[0, s - 1], {"fsdp": fz(-1)})
        if s <= AGM:
            got(ca.at[fz(s)], agr.at[1, s - 1], ags.at[1, s - 1], {"fsdp": fz(1)})
        ag_send(s)

    def dx_step(s):
        ks = [k for k, ok in ((-s, s <= AGP), (s, s <= AGM and s > 0)) if ok]
        bs = [fz(k) for k in ks]
        acc = None
        for q in range(T):
            lhs = jnp.concatenate([ca[b, q] for b in bs], axis=0) if len(bs) > 1 else ca[bs[0], q]
            p = lax.dot_general(lhs, wg[q], (((1,), (1,)), ((), ())), preferred_element_type=f32)
            acc = p if acc is None else acc + p
        for n, (k, b) in enumerate(zip(ks, bs)):
            r = acc[n * QR:(n + 1) * QR].astype(bf16)
            if k == 0:
                dx_o[:, pl.ds(pl.multiple_of(f * DB, DB), DB)] = r
            else:
                i = k % F - 1
                dxs[b] = r
                send(dxs.at[b], dx_blk(f), dxsm.at[i], dxr.at[i], {"fsdp": b})

    def y_step(s):
        for h in range(2):
            for d, hops, sgn in ((0, YP[h], 1), (1, YM[h], -1)):
                if s < hops:
                    got(yrr.at[d, h, s - 1], yrrs.at[d, h, s - 1], yrs.at[d, h, s - 1], yd(-sgn))
                    b = yy(sgn * (hops - s))
                    yss[d, h, s - 1] = (yrr[d, h, s - 1].astype(f32) + fr[b, h].astype(f32)).astype(bf16)
                    send(yss.at[d, h, s - 1], yrr.at[d, h, s], yrs.at[d, h, s], yrrs.at[d, h, s], yd(sgn))

    def y_last():
        for h in range(2):
            got(yrr.at[0, h, YP[h] - 1], yrrs.at[0, h, YP[h] - 1], yrs.at[0, h, YP[h] - 1], yd(-1))
            got(yrr.at[1, h, YM[h] - 1], yrrs.at[1, h, YM[h] - 1], yrs.at[1, h, YM[h] - 1], yd(1))
            ys[h] = (yrr[0, h, YP[h] - 1].astype(f32) + yrr[1, h, YM[h] - 1].astype(f32)
                     + fr[y, h].astype(f32)).astype(bf16)
            send(ys.at[h], xr.at[h], xss.at[h], xsr.at[h], xpart)

    def update(b, h):
        avg = ov[b, h] - sm[b, h].astype(f32) * (1.0 / (2 * Y))
        nm = beta_outer * mv[b, h] + avg
        nm_o[b, h] = nm
        no_o[b, h] = ov[b, h] - outer_rate * (avg + beta_outer * nm)

    def ya_send(s):
        for h in range(2):
            if s < YP[h]:
                b = yy(-s)
                send(sm.at[b, h], sm.at[b, h], yas.at[0, h, s], yar.at[0, h, s], yd(1))
            if s < YM[h]:
                b = yy(s)
                send(sm.at[b, h], sm.at[b, h], yas.at[1, h, s], yar.at[1, h, s], yd(-1))

    def ya_first():
        for h in range(2):
            got(xr.at[h], xsr.at[h], xss.at[h], xpart)
            sm[y, h] = (ys[h].astype(f32) + xr[h].astype(f32)).astype(bf16)
        ya_send(0)

    def upd(s):
        for h in range(2):
            if s <= YP[h]:
                update(yy(-s), h)
            if 0 < s <= YM[h]:
                update(yy(s), h)

    def ya_step(s):
        for h in range(2):
            if s <= YP[h]:
                b = yy(-s)
                got(sm.at[b, h], yar.at[0, h, s - 1], yas.at[0, h, s - 1], yd(-1))
            if s <= YM[h]:
                b = yy(s)
                got(sm.at[b, h], yar.at[1, h, s - 1], yas.at[1, h, s - 1], yd(1))
        ya_send(s)

    def k_make(s):
        ks = [k for k, ok in ((RSP - s, s <= RSP), (s - RSM, s < RSM)) if ok]
        for k in ks:
            if k == 0:
                l_x.wait()
            else:
                i = (-k) % F - 1
                got(xa.at[fz(k)], tkr.at[i], tks.at[i], {"fsdp": fz(k)})
        bs = [fz(k) for k in ks]
        lhs = jnp.concatenate([xa[b] for b in bs], axis=0) if len(bs) > 1 else xa[bs[0]]
        for q in range(T):
            r = jnp.dot(lhs, wg[q], preferred_element_type=f32)
            for n, b in enumerate(bs):
                kp[q, b] = r[n * QR:(n + 1) * QR]

    def k_step(s):
        for d, hops, sgn, rv, sd in ((0, RSP, 1, krp, ksp), (1, RSM, -1, krm, ksm)):
            if s < hops:
                b = fz(sgn * (hops - s))
                v = kp[:, b]
                if s > 0:
                    got(rv.at[s - 1], ksr.at[d, s - 1], kss.at[d, s - 1], {"fsdp": fz(-sgn)})
                    v = v + rv[s - 1].astype(f32)
                sd[s] = v.astype(bf16)
                send(sd.at[s], rv.at[s], kss.at[d, s], ksr.at[d, s], {"fsdp": fz(sgn)})

    def k_last():
        got(krp.at[RSP - 1], ksr.at[0, RSP - 1], kss.at[0, RSP - 1], {"fsdp": fz(-1)})
        got(krm.at[RSM - 1], ksr.at[1, RSM - 1], kss.at[1, RSM - 1], {"fsdp": fz(1)})
        kfin[...] = (kp[:, f] + krp[RSP - 1].astype(f32) + krm[RSM - 1].astype(f32)).astype(bf16)
        rows = pl.ds(pl.multiple_of(t * QR, QR), QR)
        mine = keys_o.at[rows, :]
        for j in range(1, T):
            q = ty(j)
            send(kfin.at[q], mine, kts.at[j - 1], ktr.at[j - 1], {"tensor": q})
        keys_o[rows, :] = kfin[t]

    far = 1 - xlo

    def w_one(q):
        r = lax.dot_general(xa[...].reshape(F * QR, DB), ca[:, q].reshape(F * QR, KT),
                            (((0,), (0,)), ((), ())), preferred_element_type=f32)
        dwp[q] = r.astype(bf16)

    def w_pair(m, i):
        w_one(2 * m + 1 - core)
        send(dwp.at[2 * m + 1 - core], dwr.at[i], dwss.at[i], dwsr.at[i], {"tensor": tc})
        w_one(2 * m + core)

    def w_mid():
        got(dwr.at[0], dwsr.at[0], dwss.at[0], {"tensor": tc})
        dws[...] = (dwp[2 * far + core].astype(f32) + dwr[0].astype(f32)).astype(bf16)
        send(dws, dwx, dwss.at[2], dwsr.at[2], {"tensor": tx})

    def w_last():
        got(dwr.at[1], dwsr.at[1], dwss.at[1], {"tensor": tc})
        got(dwx, dwsr.at[2], dwss.at[2], {"tensor": tx})
        dw_o[...] = (dwp[2 * xlo + core].astype(f32) + dwr[1].astype(f32) + dwx[...].astype(f32)).astype(bf16)

    ag_send(0)
    wave()
    tok_send((6, 5, -5, 4, -4, 3, -3, 2, -2))
    l_f.wait()
    y_step(1)
    ag_step(1)
    y_step(2)
    ag_step(2)
    got(wg.at[tx], wsr.at[0], wss.at[0], {"tensor": tx})
    send(wg.at[tx], wg.at[tx], wss.at[2], wsr.at[2], {"tensor": tc})
    l_w.wait()
    got(wg.at[tc], wsr.at[1], wss.at[1], {"tensor": tc})
    txc = lax.rem(tc + 2, T)
    got(wg.at[txc], wsr.at[2], wss.at[2], {"tensor": tc})
    k_make(0)
    k_step(0)
    dx_step(1)
    y_step(3)
    ag_step(3)
    k_make(1)
    k_step(1)
    dx_step(2)
    y_last()
    ag_step(4)
    k_make(2)
    k_step(2)
    dx_step(3)
    ya_first()
    ag_step(5)
    k_make(3)
    k_step(3)
    dx_step(4)
    ya_step(1)
    ag_step(6)
    dx_step(6)
    k_make(4)
    k_step(4)
    dx_step(5)
    k_make(5)
    w_pair(far, 0)
    ya_step(2)
    k_step(5)
    w_mid()
    ya_step(3)
    w_pair(xlo, 1)
    dx_step(0)
    k_last()
    l_o.wait()
    l_m.wait()
    for s in range(4):
        upd(s)
    ya_step(4)
    upd(4)
    w_last()
    for k in range(1, F):
        got(dx_blk(fz(-k)), dxr.at[k - 1], dxsm.at[k - 1], {"fsdp": fz(-k)})
    for j in range(1, T):
        q = ty(-j)
        got(keys_o.at[pl.ds(pl.multiple_of(q * QR, QR), QR), :], ktr.at[j - 1], kts.at[j - 1], {"tensor": q})
    for c in pending:
        c.wait_send()


def flush(*refs):
    n = len(refs) // 2
    sem = refs[-1]
    copies = [pltpu.make_async_copy(refs[i], refs[n + i], sem.at[i]) for i in (3, 4, 1, 2, 0)]
    for c in copies:
        c.start()
    for c in copies:
        c.wait()


def body(tokens, key_weight, key_cotangent, local_frag, outer_frag, momentum):
    FS = (Y, 2, 64, 512)
    V, DMA = pltpu.VMEM, pltpu.SemaphoreType.DMA
    blk = (T, QR, KT)
    hbm = pl.BlockSpec(memory_space=pltpu.HBM)
    vmem = pl.BlockSpec(memory_space=pltpu.VMEM)
    outs = (
        jax.ShapeDtypeStruct((T * QR, KT), bf16),
        jax.ShapeDtypeStruct((QR, F * DB), bf16),
        jax.ShapeDtypeStruct((DB, KT), bf16),
        jax.ShapeDtypeStruct(FS, f32),
        jax.ShapeDtypeStruct(FS, f32),
    )
    fixed = lambda a: pltpu.with_memory_space_constraint(a, pltpu.HBM)
    made = pl.pallas_call(
        kernel,
        out_shape=tuple(V(o.shape, o.dtype) for o in outs),
        in_specs=[hbm] * 6,
        out_specs=(vmem,) * 5,
        scratch_shapes=[
            V((F, QR, DB), bf16), V((F,) + blk, bf16), V((T, DB, KT), bf16), V((F, QR, DB), bf16),
            V((T, F, QR, KT), f32), V((RSP,) + blk, bf16), V((RSM,) + blk, bf16),
            V((RSP,) + blk, bf16), V((RSM,) + blk, bf16), V(blk, bf16),
            V((T, DB, KT), bf16), V((2, DB, KT), bf16), V((DB, KT), bf16), V((DB, KT), bf16),
            V(FS, bf16), V((2, 2, 3, 64, 512), bf16), V((2, 2, 4, 64, 512), bf16),
            V((2, 64, 512), bf16), V((2, 64, 512), bf16), V(FS, bf16),
            V(FS, f32), V(FS, f32),
            DMA((6,)), DMA((11,)), DMA((11,)), DMA((3,)), DMA((3,)), DMA((3,)), DMA((3,)),
            DMA((2, 6)), DMA((2, 6)), DMA((11,)), DMA((11,)), DMA((2, 6)), DMA((2, 6)), DMA((3,)), DMA((3,)),
            DMA((3,)), DMA((3,)), DMA((2, 2, 4)), DMA((2, 2, 4)), DMA((2,)), DMA((2,)),
            DMA((2, 2, 4)), DMA((2, 2, 4)), pltpu.SemaphoreType.REGULAR((2, F // 2)),
        ],
        compiler_params=pltpu.CompilerParams(collective_id=0, has_side_effects=True,
                                             vmem_limit_bytes=40 << 20),
    )(*map(fixed, (tokens, key_weight[0], key_cotangent, local_frag.reshape(FS), outer_frag.reshape(FS), momentum.reshape(FS))))
    keys, dx, dw, no, nm = pl.pallas_call(
        flush,
        out_shape=outs,
        in_specs=[vmem] * 5,
        out_specs=(hbm,) * 5,
        scratch_shapes=[DMA((5,))],
        compiler_params=pltpu.CompilerParams(vmem_limit_bytes=1 << 20),
    )(*made)
    return keys, dx, dw[None], no.reshape(outer_frag.shape), nm.reshape(momentum.shape)


def solution(mesh):
    return jax.shard_map(
        body,
        mesh=mesh,
        in_specs=(
            P(("island", "fsdp"), None),
            P("island", "fsdp", "tensor"),
            P(("island", "fsdp"), "tensor"),
            P("island", None, "fsdp", "tensor"),
            P(None, "fsdp", "tensor"),
            P(None, "fsdp", "tensor"),
        ),
        out_specs=(
            P(("island", "fsdp"), "tensor"),
            P(("island", "fsdp", "tensor"), None),
            P("island", "fsdp", "tensor"),
            P(None, "fsdp", "tensor"),
            P(None, "fsdp", "tensor"),
        ),
        check_vma=False,
    )
```

```python
import jax
import jax.numpy as jnp
from jax import lax
from jax.experimental import pallas as pl
from jax.experimental.pallas import tpu as pltpu
from jax.sharding import PartitionSpec as P

outer_rate = 0.7
beta_outer = 0.9
MESH = pl.DeviceIdType.MESH
F, T, Y = 12, 4, 8
QR, DB, KT = 32, 512, 256
bf16, f32 = jnp.bfloat16, jnp.float32


def kernel(tok, w, cot, frag, outer, mom, keys_o, dx_o, dw_o, no_o, nm_o,
           xa, ca, wg, dxs, kp, kst, kl, kf, kfin, dwp, dwr, dws, dwx,
           fr, yss, yl, yf, ys, xr, sm, ov, mv,
           lsem, tks, tkr, cts, ctr, wss, wsr, ags, agr, dxsm, dxr, kss, ksr, kts, ktr,
           dwss, dwsr, yrs, yrrs, xss, xsr, yas, yar):
    isl = lax.axis_index("island")
    f = lax.axis_index("fsdp")
    t = lax.axis_index("tensor")
    y = lax.rem(isl, Y)
    xh = isl - y
    fz = lambda k: lax.rem(f + (k + F), F)
    ty = lambda k: lax.rem(t + (k + T), T)
    yy = lambda k: lax.rem(y + (k + 2 * Y), Y)
    yd = lambda k: {"island": xh + yy(k)}
    xpart = {"island": lax.rem(isl + Y, 2 * Y)}
    core = lax.rem(t, 2)
    xlo = lax.div(t, 2)
    tc = t + 1 - 2 * core
    tx = ty(2)
    pending = []

    def local(src, dst, sem):
        c = pltpu.make_async_copy(src, dst, sem)
        c.start()
        return c

    def rc(src, dst, ss, rs, dev):
        return pltpu.make_async_remote_copy(src_ref=src, dst_ref=dst, send_sem=ss, recv_sem=rs,
                                            device_id=dev, device_id_type=MESH)

    def send(*a):
        c = rc(*a)
        c.start()
        pending.append(c)

    def got(dst, rs, ss, dev):
        rc(dst, dst, ss, rs, dev).wait_recv()

    cot_rows = lambda q: cot.at[pl.ds(pl.multiple_of(q * QR, QR), QR), :]
    tok_blk = lambda b: tok.at[pl.ds(pl.multiple_of(t * QR, QR), QR), pl.ds(pl.multiple_of(b * DB, DB), DB)]
    dx_blk = lambda b: dx_o.at[:, pl.ds(pl.multiple_of(b * DB, DB), DB)]

    bar = pltpu.get_barrier_semaphore()
    peers = [{"fsdp": fz(k)} for k in range(1, F)] + [{"tensor": ty(k)} for k in range(1, T)]
    peers += [yd(1), yd(-1), yd(2), yd(-2), xpart]
    for d in peers:
        pl.semaphore_signal(bar, inc=1, device_id=d, device_id_type=MESH)

    l_w = local(w, wg.at[t], lsem.at[0])
    l_c = local(cot_rows(t), ca.at[f, t], lsem.at[1])
    l_x = local(tok_blk(f), xa.at[f], lsem.at[2])
    l_f = local(frag, fr, lsem.at[3])
    pl.semaphore_wait(bar, len(peers))

    for j in range(1, T):
        send(cot_rows(ty(j)), ca.at[f, t], cts.at[j - 1], ctr.at[j - 1], {"tensor": ty(j)})
    for h in range(2):
        four = 2 if h == 0 else -2
        send(frag.at[yy(4), h], yl.at[h, 2], yrs.at[h, 2], yrrs.at[h, 2], yd(four))
        send(frag.at[yy(3), h], yl.at[h, 0], yrs.at[h, 0], yrrs.at[h, 0], yd(1))
        send(frag.at[yy(-3), h], yl.at[h, 1], yrs.at[h, 1], yrrs.at[h, 1], yd(-1))
    for h in range(2):
        send(frag.at[yy(1), h], yf.at[h, 0], yrs.at[h, 3], yrrs.at[h, 3], yd(1))
        send(frag.at[yy(-1), h], yf.at[h, 1], yrs.at[h, 4], yrrs.at[h, 4], yd(-1))
    send(w, wg.at[t], wss.at[0], wsr.at[0], {"tensor": tx})
    send(w, wg.at[t], wss.at[1], wsr.at[1], {"tensor": tc})
    def tok_send(ks):
        for k in ks:
            b = fz(k)
            i = k % F - 1
            send(tok_blk(b), xa.at[f], tks.at[i], tkr.at[i], {"fsdp": b})

    tok_send((6, 5, -5))
    l_o = local(outer, ov, lsem.at[4])
    l_m = local(mom, mv, lsem.at[5])

    l_c.wait()
    for j in range(1, T):
        got(ca.at[f, ty(-j)], ctr.at[j - 1], cts.at[j - 1], {"tensor": ty(-j)})

    sg = 1 - 2 * core

    def ag_put(b, k, to):
        i = k % F - 1
        send(ca.at[b], ca.at[b], ags.at[i], agr.at[i], {"fsdp": fz(to)})

    def ag_got(*ks):
        for k in ks:
            i = k % F - 1
            got(ca.at[fz(-k)], agr.at[i], ags.at[i], {"fsdp": fz(-k)})

    def ag_first():
        for k in (3, -3, 2, -2, 1, -1):
            ag_put(f, k, k)

    def ag_pass():
        ag_got(3, -3)
        ag_put(fz(-3 * sg), 6, 3 * sg)
        for k in (5, -5, 4, -4):
            d = 3 if k > 0 else -3
            ag_put(fz(-d), k, k - d)

    def dx_step(s):
        ks = (-s, s) if s % 6 else (s,)
        bs = [fz(k) for k in ks]
        acc = None
        for q in range(T):
            lhs = jnp.concatenate([ca[b, q] for b in bs], axis=0) if len(bs) > 1 else ca[bs[0], q]
            p = lax.dot_general(lhs, wg[q], (((1,), (1,)), ((), ())), preferred_element_type=f32)
            acc = p if acc is None else acc + p
        for n, (k, b) in enumerate(zip(ks, bs)):
            r = acc[n * QR:(n + 1) * QR].astype(bf16)
            if k == 0:
                dx_o[:, pl.ds(pl.multiple_of(f * DB, DB), DB)] = r
            else:
                i = k % F - 1
                dxs[b] = r
                send(dxs.at[b], dx_blk(f), dxsm.at[i], dxr.at[i], {"fsdp": b})

    def y_got(ref, h, i):
        got(ref, yrrs.at[h, i], yrs.at[h, i], yd(1))
        return ref[...].astype(f32)

    def y_relay():
        for h in range(2):
            four = y_got(yl.at[h, 2], h, 2)
            for d, sgn in ((0, 1), (1, -1)):
                v = y_got(yl.at[h, d], h, d) + fr[yy(2 * sgn), h].astype(f32)
                if d == h:
                    v = v + four
                yss[h, d] = v.astype(bf16)
                send(yss.at[h, d], yf.at[h, 2 + d], yrs.at[h, 5 + d], yrrs.at[h, 5 + d], yd(2 * sgn))

    def y_last():
        for h in range(2):
            v = fr[y, h].astype(f32)
            for n in range(4):
                v = v + y_got(yf.at[h, n], h, 3 + n)
            ys[h] = v.astype(bf16)
            send(ys.at[h], xr.at[h], xss.at[h], xsr.at[h], xpart)

    def update(b, h):
        avg = ov[b, h] - sm[b, h].astype(f32) * (1.0 / (2 * Y))
        nm = beta_outer * mv[b, h] + avg
        nm_o[b, h] = nm
        no_o[b, h] = ov[b, h] - outer_rate * (avg + beta_outer * nm)

    def ya_put(b, h, k, to):
        i = k % Y - 1
        send(sm.at[b, h], sm.at[b, h], yas.at[h, i], yar.at[h, i], yd(to))

    def ya_got(h, k):
        i = k % Y - 1
        got(sm.at[yy(-k), h], yar.at[h, i], yas.at[h, i], yd(1))

    def ya_first():
        for h in range(2):
            got(xr.at[h], xsr.at[h], xss.at[h], xpart)
            sm[y, h] = (ys[h].astype(f32) + xr[h].astype(f32)).astype(bf16)
            for k in (2, -2, 1, -1):
                ya_put(y, h, k, k)

    def ya_pass():
        for h in range(2):
            ya_got(h, 2)
            ya_got(h, -2)
            ya_put(yy(-2 if h == 0 else 2), h, 4, 2 if h == 0 else -2)
            ya_put(yy(-2), h, 3, 1)
            ya_put(yy(2), h, -3, -1)

    def upd(*ks):
        for h in range(2):
            for k in ks:
                if k not in (0, 2, -2):
                    ya_got(h, k)
                update(yy(-k), h)

    def k_make(*ks):
        for k in ks:
            if k == 0:
                l_x.wait()
            else:
                i = (-k) % F - 1
                got(xa.at[fz(k)], tkr.at[i], tks.at[i], {"fsdp": fz(k)})
        bs = [fz(k) for k in ks]
        lhs = jnp.concatenate([xa[b] for b in bs], axis=0) if len(bs) > 1 else xa[bs[0]]
        for q in range(T):
            r = jnp.dot(lhs, wg[q], preferred_element_type=f32)
            for n, k in enumerate(ks):
                v = r[n * QR:(n + 1) * QR]
                if k in (0, 3, -3):
                    kp[q, (0, 3, -3).index(k)] = v
                else:
                    kst[k % F, q] = v.astype(bf16)

    def k_leaf():
        k_make(6)
        send(kst.at[6], kl.at[2, 0], kss.at[6], ksr.at[6], {"fsdp": fz(3 * sg)})
        for j in (2, 1):
            k_make(3 + j, -3 - j)
            for d, sgn in ((0, 1), (1, -1)):
                k = sgn * (3 + j)
                send(kst.at[k % F], kl.at[d, j - 1], kss.at[k % F], ksr.at[k % F], {"fsdp": fz(sgn * j)})

    def k_near(j):
        k_make(j, -j)
        for d, sgn in ((0, 1), (1, -1)):
            k = sgn * j
            send(kst.at[k % F], kf.at[d, j - 1], kss.at[k % F], ksr.at[k % F], {"fsdp": fz(k)})

    def k_relay():
        got(kl.at[2, 0], ksr.at[6], kss.at[6], {"fsdp": fz(-3)})
        for d, sgn in ((0, 1), (1, -1)):
            v = kp[:, 1 + d]
            for j in (1, 2):
                k = (sgn * (3 + j)) % F
                got(kl.at[d, j - 1], ksr.at[k], kss.at[k], {"fsdp": fz(-sgn * j)})
                v = v + kl[d, j - 1].astype(f32)
            here = (core == d).astype(f32)
            v = v + here * kl[2, 0].astype(f32)
            k = (3 * sgn) % F
            kst[k] = v.astype(bf16)
            send(kst.at[k], kf.at[d, 2], kss.at[k], ksr.at[k], {"fsdp": fz(3 * sgn)})

    def k_last():
        v = kp[:, 0]
        for j in (1, 2, 3):
            for d, sgn in ((0, 1), (1, -1)):
                k = (sgn * j) % F
                got(kf.at[d, j - 1], ksr.at[k], kss.at[k], {"fsdp": fz(-sgn * j)})
                v = v + kf[d, j - 1].astype(f32)
        kfin[...] = v.astype(bf16)
        rows = pl.ds(pl.multiple_of(t * QR, QR), QR)
        mine = keys_o.at[rows, :]
        for j in range(1, T):
            q = ty(j)
            send(kfin.at[q], mine, kts.at[j - 1], ktr.at[j - 1], {"tensor": q})
        keys_o[rows, :] = kfin[t]

    far = 1 - xlo

    def w_one(q):
        r = lax.dot_general(xa[...].reshape(F * QR, DB), ca[:, q].reshape(F * QR, KT),
                            (((0,), (0,)), ((), ())), preferred_element_type=f32)
        dwp[q] = r.astype(bf16)

    def w_pair(m, i):
        w_one(2 * m + 1 - core)
        send(dwp.at[2 * m + 1 - core], dwr.at[i], dwss.at[i], dwsr.at[i], {"tensor": tc})
        w_one(2 * m + core)

    def w_mid():
        got(dwr.at[0], dwsr.at[0], dwss.at[0], {"tensor": tc})
        dws[...] = (dwp[2 * far + core].astype(f32) + dwr[0].astype(f32)).astype(bf16)
        send(dws, dwx, dwss.at[2], dwsr.at[2], {"tensor": tx})

    def w_last():
        got(dwr.at[1], dwsr.at[1], dwss.at[1], {"tensor": tc})
        got(dwx, dwsr.at[2], dwss.at[2], {"tensor": tx})
        dw_o[...] = (dwp[2 * xlo + core].astype(f32) + dwr[1].astype(f32) + dwx[...].astype(f32)).astype(bf16)

    ag_first()
    tok_send((4, -4, 3, -3))
    l_f.wait()
    y_relay()
    ag_pass()
    tok_send((2, -2, 1, -1))
    got(wg.at[tx], wsr.at[0], wss.at[0], {"tensor": tx})
    send(wg.at[tx], wg.at[tx], wss.at[2], wsr.at[2], {"tensor": tc})
    l_w.wait()
    got(wg.at[tc], wsr.at[1], wss.at[1], {"tensor": tc})
    txc = lax.rem(tc + 2, T)
    got(wg.at[txc], wsr.at[2], wss.at[2], {"tensor": tc})
    k_leaf()
    y_last()
    dx_step(3)
    k_make(3, -3)
    ag_got(2, -2, 1, -1)
    k_relay()
    dx_step(2)
    k_near(2)
    ya_first()
    k_near(1)
    dx_step(1)
    ag_got(6, 5, -5, 4, -4)
    dx_step(6)
    dx_step(5)
    dx_step(4)
    k_make(0)
    w_pair(far, 0)
    ya_pass()
    k_last()
    w_mid()
    w_pair(xlo, 1)
    dx_step(0)
    l_o.wait()
    l_m.wait()
    upd(0, 2, -2)
    upd(1, -1)
    upd(3, -3)
    upd(4)
    w_last()
    for k in range(1, F):
        got(dx_blk(fz(-k)), dxr.at[k - 1], dxsm.at[k - 1], {"fsdp": fz(-k)})
    for j in range(1, T):
        q = ty(-j)
        got(keys_o.at[pl.ds(pl.multiple_of(q * QR, QR), QR), :], ktr.at[j - 1], kts.at[j - 1], {"tensor": q})
    for c in pending:
        c.wait_send()


def flush(*refs):
    n = len(refs) // 2
    sem = refs[-1]
    copies = [pltpu.make_async_copy(refs[i], refs[n + i], sem.at[i]) for i in (3, 4, 1, 2, 0)]
    for c in copies:
        c.start()
    for c in copies:
        c.wait()


def body(tokens, key_weight, key_cotangent, local_frag, outer_frag, momentum):
    FS = (Y, 2, 64, 512)
    V, DMA = pltpu.VMEM, pltpu.SemaphoreType.DMA
    blk = (T, QR, KT)
    hbm = pl.BlockSpec(memory_space=pltpu.HBM)
    vmem = pl.BlockSpec(memory_space=pltpu.VMEM)
    outs = (
        jax.ShapeDtypeStruct((T * QR, KT), bf16),
        jax.ShapeDtypeStruct((QR, F * DB), bf16),
        jax.ShapeDtypeStruct((DB, KT), bf16),
        jax.ShapeDtypeStruct(FS, f32),
        jax.ShapeDtypeStruct(FS, f32),
    )
    fixed = lambda a: pltpu.with_memory_space_constraint(a, pltpu.HBM)
    made = pl.pallas_call(
        kernel,
        out_shape=tuple(V(o.shape, o.dtype) for o in outs),
        in_specs=[hbm] * 6,
        out_specs=(vmem,) * 5,
        scratch_shapes=[
            V((F, QR, DB), bf16), V((F,) + blk, bf16), V((T, DB, KT), bf16), V((F, QR, DB), bf16),
            V((T, 3, QR, KT), f32), V((F,) + blk, bf16), V((3, 2) + blk, bf16), V((2, 3) + blk, bf16), V(blk, bf16),
            V((T, DB, KT), bf16), V((2, DB, KT), bf16), V((DB, KT), bf16), V((DB, KT), bf16),
            V(FS, bf16), V((2, 2, 64, 512), bf16), V((2, 3, 64, 512), bf16), V((2, 4, 64, 512), bf16),
            V((2, 64, 512), bf16), V((2, 64, 512), bf16), V(FS, bf16),
            V(FS, f32), V(FS, f32),
            DMA((6,)), DMA((11,)), DMA((11,)), DMA((3,)), DMA((3,)), DMA((3,)), DMA((3,)),
            DMA((11,)), DMA((11,)), DMA((11,)), DMA((11,)), DMA((F,)), DMA((F,)), DMA((3,)), DMA((3,)),
            DMA((3,)), DMA((3,)), DMA((2, 7)), DMA((2, 7)), DMA((2,)), DMA((2,)),
            DMA((2, 7)), DMA((2, 7)),
        ],
        compiler_params=pltpu.CompilerParams(collective_id=0, has_side_effects=True,
                                             vmem_limit_bytes=40 << 20),
    )(*map(fixed, (tokens, key_weight[0], key_cotangent, local_frag.reshape(FS), outer_frag.reshape(FS), momentum.reshape(FS))))
    keys, dx, dw, no, nm = pl.pallas_call(
        flush,
        out_shape=outs,
        in_specs=[vmem] * 5,
        out_specs=(hbm,) * 5,
        scratch_shapes=[DMA((5,))],
        compiler_params=pltpu.CompilerParams(vmem_limit_bytes=1 << 20),
    )(*made)
    return keys, dx, dw[None], no.reshape(outer_frag.shape), nm.reshape(momentum.shape)


def solution(mesh):
    return jax.shard_map(
        body,
        mesh=mesh,
        in_specs=(
            P(("island", "fsdp"), None),
            P("island", "fsdp", "tensor"),
            P(("island", "fsdp"), "tensor"),
            P("island", None, "fsdp", "tensor"),
            P(None, "fsdp", "tensor"),
            P(None, "fsdp", "tensor"),
        ),
        out_specs=(
            P(("island", "fsdp"), "tensor"),
            P(("island", "fsdp", "tensor"), None),
            P("island", "fsdp", "tensor"),
            P(None, "fsdp", "tensor"),
            P(None, "fsdp", "tensor"),
        ),
        check_vma=False,
    )
```

```python
import jax
import jax.numpy as jnp
from jax import lax
from jax.experimental import pallas as pl
from jax.experimental.pallas import tpu as pltpu
from jax.sharding import PartitionSpec as P

outer_rate = 0.7
beta_outer = 0.9
MESH = pl.DeviceIdType.MESH
F, T, Y = 12, 4, 8
QR, DB, KT = 32, 512, 256
AGP, AGM = 6, 5
RSP, RSM = 5, 6
YP = (4, 3)
YM = (3, 4)
bf16, f32 = jnp.bfloat16, jnp.float32


def kernel(tok, w, cot, frag, outer, mom, keys_o, dx_o, dw_o, no_o, nm_o,
           xa, ca, wg, dxs, kp, ksp, ksm, krp, krm, kfin, dwp, dwr, dws, dwx,
           fr, yss, yrr, ys, xr, sm, ov, mv,
           lsem, tks, tkr, cts, ctr, wss, wsr, ags, agr, dxsm, dxr, kss, ksr, kts, ktr,
           dwss, dwsr, yrs, yrrs, xss, xsr, yas, yar):
    isl = lax.axis_index("island")
    f = lax.axis_index("fsdp")
    t = lax.axis_index("tensor")
    y = lax.rem(isl, Y)
    xh = isl - y
    fz = lambda k: lax.rem(f + (k + F), F)
    ty = lambda k: lax.rem(t + (k + T), T)
    yy = lambda k: lax.rem(y + (k + 2 * Y), Y)
    yd = lambda k: {"island": xh + yy(k)}
    xpart = {"island": lax.rem(isl + Y, 2 * Y)}
    core = lax.rem(t, 2)
    xlo = lax.div(t, 2)
    tc = t + 1 - 2 * core
    tx = ty(2)
    pending = []

    def local(src, dst, sem):
        c = pltpu.make_async_copy(src, dst, sem)
        c.start()
        return c

    def rc(src, dst, ss, rs, dev):
        return pltpu.make_async_remote_copy(src_ref=src, dst_ref=dst, send_sem=ss, recv_sem=rs,
                                            device_id=dev, device_id_type=MESH)

    def send(*a):
        c = rc(*a)
        c.start()
        pending.append(c)

    def got(dst, rs, ss, dev):
        rc(dst, dst, ss, rs, dev).wait_recv()

    cot_rows = lambda q: cot.at[pl.ds(pl.multiple_of(q * QR, QR), QR), :]
    tok_blk = lambda b: tok.at[pl.ds(pl.multiple_of(t * QR, QR), QR), pl.ds(pl.multiple_of(b * DB, DB), DB)]
    dx_blk = lambda b: dx_o.at[:, pl.ds(pl.multiple_of(b * DB, DB), DB)]

    bar = pltpu.get_barrier_semaphore()
    peers = [{"fsdp": fz(k)} for k in range(1, F)] + [{"tensor": ty(k)} for k in range(1, T)]
    peers += [yd(1), yd(-1), xpart]
    for d in peers:
        pl.semaphore_signal(bar, inc=1, device_id=d, device_id_type=MESH)

    l_w = local(w, wg.at[t], lsem.at[0])
    l_c = local(cot_rows(t), ca.at[f, t], lsem.at[1])
    l_x = local(tok_blk(f), xa.at[f], lsem.at[2])
    l_f = local(frag, fr, lsem.at[3])
    pl.semaphore_wait(bar, len(peers))

    for j in range(1, T):
        send(cot_rows(ty(j)), ca.at[f, t], cts.at[j - 1], ctr.at[j - 1], {"tensor": ty(j)})
    for h in range(2):
        send(frag.at[yy(YP[h]), h], yrr.at[0, h, 0], yrs.at[0, h, 0], yrrs.at[0, h, 0], yd(1))
        send(frag.at[yy(-YM[h]), h], yrr.at[1, h, 0], yrs.at[1, h, 0], yrrs.at[1, h, 0], yd(-1))
    send(w, wg.at[t], wss.at[0], wsr.at[0], {"tensor": tx})
    send(w, wg.at[t], wss.at[1], wsr.at[1], {"tensor": tc})
    def tok_send(ks):
        for k in ks:
            b = fz(k)
            i = k % F - 1
            send(tok_blk(b), xa.at[f], tks.at[i], tkr.at[i], {"fsdp": b})

    tok_send((6, 5, -5))
    l_o = local(outer, ov, lsem.at[4])
    l_m = local(mom, mv, lsem.at[5])

    l_c.wait()
    for j in range(1, T):
        got(ca.at[f, ty(-j)], ctr.at[j - 1], cts.at[j - 1], {"tensor": ty(-j)})

    def ag_send(s):
        if s < AGP:
            b = fz(-s)
            send(ca.at[b], ca.at[b], ags.at[0, s], agr.at[0, s], {"fsdp": fz(1)})
        if s < AGM:
            b = fz(s)
            send(ca.at[b], ca.at[b], ags.at[1, s], agr.at[1, s], {"fsdp": fz(-1)})

    def ag_step(s):
        if s <= AGP:
            got(ca.at[fz(-s)], agr.at[0, s - 1], ags.at[0, s - 1], {"fsdp": fz(-1)})
        if s <= AGM:
            got(ca.at[fz(s)], agr.at[1, s - 1], ags.at[1, s - 1], {"fsdp": fz(1)})
        ag_send(s)

    def dx_step(s):
        ks = [k for k, ok in ((-s, s <= AGP), (s, s <= AGM and s > 0)) if ok]
        bs = [fz(k) for k in ks]
        acc = None
        for q in range(T):
            lhs = jnp.concatenate([ca[b, q] for b in bs], axis=0) if len(bs) > 1 else ca[bs[0], q]
            p = lax.dot_general(lhs, wg[q], (((1,), (1,)), ((), ())), preferred_element_type=f32)
            acc = p if acc is None else acc + p
        for n, (k, b) in enumerate(zip(ks, bs)):
            r = acc[n * QR:(n + 1) * QR].astype(bf16)
            if k == 0:
                dx_o[:, pl.ds(pl.multiple_of(f * DB, DB), DB)] = r
            else:
                i = k % F - 1
                dxs[b] = r
                send(dxs.at[b], dx_blk(f), dxsm.at[i], dxr.at[i], {"fsdp": b})

    def y_step(s):
        for h in range(2):
            for d, hops, sgn in ((0, YP[h], 1), (1, YM[h], -1)):
                if s < hops:
                    got(yrr.at[d, h, s - 1], yrrs.at[d, h, s - 1], yrs.at[d, h, s - 1], yd(-sgn))
                    b = yy(sgn * (hops - s))
                    yss[d, h, s - 1] = (yrr[d, h, s - 1].astype(f32) + fr[b, h].astype(f32)).astype(bf16)
                    send(yss.at[d, h, s - 1], yrr.at[d, h, s], yrs.at[d, h, s], yrrs.at[d, h, s], yd(sgn))

    def y_last():
        for h in range(2):
            got(yrr.at[0, h, YP[h] - 1], yrrs.at[0, h, YP[h] - 1], yrs.at[0, h, YP[h] - 1], yd(-1))
            got(yrr.at[1, h, YM[h] - 1], yrrs.at[1, h, YM[h] - 1], yrs.at[1, h, YM[h] - 1], yd(1))
            ys[h] = (yrr[0, h, YP[h] - 1].astype(f32) + yrr[1, h, YM[h] - 1].astype(f32)
                     + fr[y, h].astype(f32)).astype(bf16)
            send(ys.at[h], xr.at[h], xss.at[h], xsr.at[h], xpart)

    def update(b, h):
        avg = ov[b, h] - sm[b, h].astype(f32) * (1.0 / (2 * Y))
        nm = beta_outer * mv[b, h] + avg
        nm_o[b, h] = nm
        no_o[b, h] = ov[b, h] - outer_rate * (avg + beta_outer * nm)

    def ya_send(s):
        for h in range(2):
            if s < YP[h]:
                b = yy(-s)
                send(sm.at[b, h], sm.at[b, h], yas.at[0, h, s], yar.at[0, h, s], yd(1))
            if s < YM[h]:
                b = yy(s)
                send(sm.at[b, h], sm.at[b, h], yas.at[1, h, s], yar.at[1, h, s], yd(-1))

    def ya_first():
        for h in range(2):
            got(xr.at[h], xsr.at[h], xss.at[h], xpart)
            sm[y, h] = (ys[h].astype(f32) + xr[h].astype(f32)).astype(bf16)
        ya_send(0)

    def upd(s):
        for h in range(2):
            if s <= YP[h]:
                update(yy(-s), h)
            if 0 < s <= YM[h]:
                update(yy(s), h)

    def ya_step(s):
        for h in range(2):
            if s <= YP[h]:
                b = yy(-s)
                got(sm.at[b, h], yar.at[0, h, s - 1], yas.at[0, h, s - 1], yd(-1))
            if s <= YM[h]:
                b = yy(s)
                got(sm.at[b, h], yar.at[1, h, s - 1], yas.at[1, h, s - 1], yd(1))
        ya_send(s)

    def k_make(s):
        ks = [k for k, ok in ((RSP - s, s <= RSP), (s - RSM, s < RSM)) if ok]
        for k in ks:
            if k == 0:
                l_x.wait()
            else:
                i = (-k) % F - 1
                got(xa.at[fz(k)], tkr.at[i], tks.at[i], {"fsdp": fz(k)})
        bs = [fz(k) for k in ks]
        lhs = jnp.concatenate([xa[b] for b in bs], axis=0) if len(bs) > 1 else xa[bs[0]]
        for q in range(T):
            r = jnp.dot(lhs, wg[q], preferred_element_type=f32)
            for n, b in enumerate(bs):
                kp[q, b] = r[n * QR:(n + 1) * QR]

    def k_step(s):
        for d, hops, sgn, rv, sd in ((0, RSP, 1, krp, ksp), (1, RSM, -1, krm, ksm)):
            if s < hops:
                b = fz(sgn * (hops - s))
                v = kp[:, b]
                if s > 0:
                    got(rv.at[s - 1], ksr.at[d, s - 1], kss.at[d, s - 1], {"fsdp": fz(-sgn)})
                    v = v + rv[s - 1].astype(f32)
                sd[s] = v.astype(bf16)
                send(sd.at[s], rv.at[s], kss.at[d, s], ksr.at[d, s], {"fsdp": fz(sgn)})

    def k_last():
        got(krp.at[RSP - 1], ksr.at[0, RSP - 1], kss.at[0, RSP - 1], {"fsdp": fz(-1)})
        got(krm.at[RSM - 1], ksr.at[1, RSM - 1], kss.at[1, RSM - 1], {"fsdp": fz(1)})
        kfin[...] = (kp[:, f] + krp[RSP - 1].astype(f32) + krm[RSM - 1].astype(f32)).astype(bf16)
        rows = pl.ds(pl.multiple_of(t * QR, QR), QR)
        mine = keys_o.at[rows, :]
        for j in range(1, T):
            q = ty(j)
            send(kfin.at[q], mine, kts.at[j - 1], ktr.at[j - 1], {"tensor": q})
        keys_o[rows, :] = kfin[t]

    far = 1 - xlo

    def w_one(q):
        r = lax.dot_general(xa[...].reshape(F * QR, DB), ca[:, q].reshape(F * QR, KT),
                            (((0,), (0,)), ((), ())), preferred_element_type=f32)
        dwp[q] = r.astype(bf16)

    def w_pair(m, i):
        w_one(2 * m + 1 - core)
        send(dwp.at[2 * m + 1 - core], dwr.at[i], dwss.at[i], dwsr.at[i], {"tensor": tc})
        w_one(2 * m + core)

    def w_mid():
        got(dwr.at[0], dwsr.at[0], dwss.at[0], {"tensor": tc})
        dws[...] = (dwp[2 * far + core].astype(f32) + dwr[0].astype(f32)).astype(bf16)
        send(dws, dwx, dwss.at[2], dwsr.at[2], {"tensor": tx})

    def w_last():
        got(dwr.at[1], dwsr.at[1], dwss.at[1], {"tensor": tc})
        got(dwx, dwsr.at[2], dwss.at[2], {"tensor": tx})
        dw_o[...] = (dwp[2 * xlo + core].astype(f32) + dwr[1].astype(f32) + dwx[...].astype(f32)).astype(bf16)

    ag_send(0)
    tok_send((4, -4, 3, -3))
    l_f.wait()
    y_step(1)
    ag_step(1)
    tok_send((2, -2, 1, -1))
    y_step(2)
    ag_step(2)
    got(wg.at[tx], wsr.at[0], wss.at[0], {"tensor": tx})
    send(wg.at[tx], wg.at[tx], wss.at[2], wsr.at[2], {"tensor": tc})
    l_w.wait()
    got(wg.at[tc], wsr.at[1], wss.at[1], {"tensor": tc})
    txc = lax.rem(tc + 2, T)
    got(wg.at[txc], wsr.at[2], wss.at[2], {"tensor": tc})
    k_make(0)
    k_step(0)
    dx_step(1)
    y_step(3)
    ag_step(3)
    k_make(1)
    k_step(1)
    dx_step(2)
    y_last()
    ag_step(4)
    k_make(2)
    k_step(2)
    dx_step(3)
    ya_first()
    ag_step(5)
    k_make(3)
    k_step(3)
    dx_step(4)
    ya_step(1)
    ag_step(6)
    dx_step(6)
    k_make(4)
    k_step(4)
    dx_step(5)
    k_make(5)
    w_pair(far, 0)
    ya_step(2)
    k_step(5)
    w_mid()
    ya_step(3)
    w_pair(xlo, 1)
    dx_step(0)
    k_last()
    l_o.wait()
    l_m.wait()
    for s in range(4):
        upd(s)
    ya_step(4)
    upd(4)
    w_last()
    for k in range(1, F):
        got(dx_blk(fz(-k)), dxr.at[k - 1], dxsm.at[k - 1], {"fsdp": fz(-k)})
    for j in range(1, T):
        q = ty(-j)
        got(keys_o.at[pl.ds(pl.multiple_of(q * QR, QR), QR), :], ktr.at[j - 1], kts.at[j - 1], {"tensor": q})
    for c in pending:
        c.wait_send()


def flush(*refs):
    n = len(refs) // 2
    sem = refs[-1]
    copies = [pltpu.make_async_copy(refs[i], refs[n + i], sem.at[i]) for i in (3, 4, 1, 2, 0)]
    for c in copies:
        c.start()
    for c in copies:
        c.wait()


def body(tokens, key_weight, key_cotangent, local_frag, outer_frag, momentum):
    FS = (Y, 2, 64, 512)
    V, DMA = pltpu.VMEM, pltpu.SemaphoreType.DMA
    blk = (T, QR, KT)
    hbm = pl.BlockSpec(memory_space=pltpu.HBM)
    vmem = pl.BlockSpec(memory_space=pltpu.VMEM)
    outs = (
        jax.ShapeDtypeStruct((T * QR, KT), bf16),
        jax.ShapeDtypeStruct((QR, F * DB), bf16),
        jax.ShapeDtypeStruct((DB, KT), bf16),
        jax.ShapeDtypeStruct(FS, f32),
        jax.ShapeDtypeStruct(FS, f32),
    )
    fixed = lambda a: pltpu.with_memory_space_constraint(a, pltpu.HBM)
    made = pl.pallas_call(
        kernel,
        out_shape=tuple(V(o.shape, o.dtype) for o in outs),
        in_specs=[hbm] * 6,
        out_specs=(vmem,) * 5,
        scratch_shapes=[
            V((F, QR, DB), bf16), V((F,) + blk, bf16), V((T, DB, KT), bf16), V((F, QR, DB), bf16),
            V((T, F, QR, KT), f32), V((RSP,) + blk, bf16), V((RSM,) + blk, bf16),
            V((RSP,) + blk, bf16), V((RSM,) + blk, bf16), V(blk, bf16),
            V((T, DB, KT), bf16), V((2, DB, KT), bf16), V((DB, KT), bf16), V((DB, KT), bf16),
            V(FS, bf16), V((2, 2, 3, 64, 512), bf16), V((2, 2, 4, 64, 512), bf16),
            V((2, 64, 512), bf16), V((2, 64, 512), bf16), V(FS, bf16),
            V(FS, f32), V(FS, f32),
            DMA((6,)), DMA((11,)), DMA((11,)), DMA((3,)), DMA((3,)), DMA((3,)), DMA((3,)),
            DMA((2, 6)), DMA((2, 6)), DMA((11,)), DMA((11,)), DMA((2, 6)), DMA((2, 6)), DMA((3,)), DMA((3,)),
            DMA((3,)), DMA((3,)), DMA((2, 2, 4)), DMA((2, 2, 4)), DMA((2,)), DMA((2,)),
            DMA((2, 2, 4)), DMA((2, 2, 4)),
        ],
        compiler_params=pltpu.CompilerParams(collective_id=0, has_side_effects=True,
                                             vmem_limit_bytes=40 << 20),
    )(*map(fixed, (tokens, key_weight[0], key_cotangent, local_frag.reshape(FS), outer_frag.reshape(FS), momentum.reshape(FS))))
    keys, dx, dw, no, nm = pl.pallas_call(
        flush,
        out_shape=outs,
        in_specs=[vmem] * 5,
        out_specs=(hbm,) * 5,
        scratch_shapes=[DMA((5,))],
        compiler_params=pltpu.CompilerParams(vmem_limit_bytes=1 << 20),
    )(*made)
    return keys, dx, dw[None], no.reshape(outer_frag.shape), nm.reshape(momentum.shape)


def solution(mesh):
    return jax.shard_map(
        body,
        mesh=mesh,
        in_specs=(
            P(("island", "fsdp"), None),
            P("island", "fsdp", "tensor"),
            P(("island", "fsdp"), "tensor"),
            P("island", None, "fsdp", "tensor"),
            P(None, "fsdp", "tensor"),
            P(None, "fsdp", "tensor"),
        ),
        out_specs=(
            P(("island", "fsdp"), "tensor"),
            P(("island", "fsdp", "tensor"), None),
            P("island", "fsdp", "tensor"),
            P(None, "fsdp", "tensor"),
            P(None, "fsdp", "tensor"),
        ),
        check_vma=False,
    )
```

```python
import jax
import jax.numpy as jnp
from jax import lax
from jax.experimental import pallas as pl
from jax.experimental.pallas import tpu as pltpu
from jax.sharding import PartitionSpec as P

outer_rate = 0.7
beta_outer = 0.9
MESH = pl.DeviceIdType.MESH
F, T, Y = 12, 4, 8
QR, DB, KT = 32, 512, 256
AGP, AGM = 6, 5
RSP, RSM = 5, 6
YP = (4, 3)
YM = (3, 4)
bf16, f32 = jnp.bfloat16, jnp.float32


def kernel(tok, w, cot, frag, outer, mom, keys_o, dx_o, dw_o, no_o, nm_o,
           xa, ca, wg, dxs, kp, ksp, ksm, krp, krm, kfin, dwp, dwr, dws, dwx,
           fr, yss, yrr, ys, xr, sm, ov, mv,
           lsem, tks, tkr, cts, ctr, wss, wsr, ags, agr, dxsm, dxr, kss, ksr, kts, ktr,
           dwss, dwsr, yrs, yrrs, xss, xsr, yas, yar):
    isl = lax.axis_index("island")
    f = lax.axis_index("fsdp")
    t = lax.axis_index("tensor")
    y = lax.rem(isl, Y)
    xh = isl - y
    fz = lambda k: lax.rem(f + (k + F), F)
    ty = lambda k: lax.rem(t + (k + T), T)
    yy = lambda k: lax.rem(y + (k + 2 * Y), Y)
    yd = lambda k: {"island": xh + yy(k)}
    xpart = {"island": lax.rem(isl + Y, 2 * Y)}
    core = lax.rem(t, 2)
    xlo = lax.div(t, 2)
    tc = t + 1 - 2 * core
    tx = ty(2)
    pending = []

    def local(src, dst, sem):
        c = pltpu.make_async_copy(src, dst, sem)
        c.start()
        return c

    def rc(src, dst, ss, rs, dev):
        return pltpu.make_async_remote_copy(src_ref=src, dst_ref=dst, send_sem=ss, recv_sem=rs,
                                            device_id=dev, device_id_type=MESH)

    def send(*a):
        c = rc(*a)
        c.start()
        pending.append(c)

    def got(dst, rs, ss, dev):
        rc(dst, dst, ss, rs, dev).wait_recv()

    cot_rows = lambda q: cot.at[pl.ds(pl.multiple_of(q * QR, QR), QR), :]
    tok_blk = lambda b: tok.at[pl.ds(pl.multiple_of(t * QR, QR), QR), pl.ds(pl.multiple_of(b * DB, DB), DB)]
    dx_blk = lambda b: dx_o.at[:, pl.ds(pl.multiple_of(b * DB, DB), DB)]

    bar = pltpu.get_barrier_semaphore()
    peers = [{"fsdp": fz(k)} for k in range(1, F)] + [{"tensor": ty(k)} for k in range(1, T)]
    peers += [yd(1), yd(-1), xpart]
    for d in peers:
        pl.semaphore_signal(bar, inc=1, device_id=d, device_id_type=MESH)

    l_w = local(w, wg.at[t], lsem.at[0])
    l_c = local(cot_rows(t), ca.at[f, t], lsem.at[1])
    l_x = local(tok_blk(f), xa.at[f], lsem.at[2])
    l_f = local(frag, fr, lsem.at[3])
    pl.semaphore_wait(bar, len(peers))

    for j in range(1, T):
        send(cot_rows(ty(j)), ca.at[f, t], cts.at[j - 1], ctr.at[j - 1], {"tensor": ty(j)})
    for h in range(2):
        send(frag.at[yy(YP[h]), h], yrr.at[0, h, 0], yrs.at[0, h, 0], yrrs.at[0, h, 0], yd(1))
        send(frag.at[yy(-YM[h]), h], yrr.at[1, h, 0], yrs.at[1, h, 0], yrrs.at[1, h, 0], yd(-1))
    send(w, wg.at[t], wss.at[0], wsr.at[0], {"tensor": tx})
    send(w, wg.at[t], wss.at[1], wsr.at[1], {"tensor": tc})
    def tok_send(ks):
        for k in ks:
            b = fz(k)
            i = k % F - 1
            send(tok_blk(b), xa.at[f], tks.at[i], tkr.at[i], {"fsdp": b})

    tok_send((6, 5, -5))
    l_o = local(outer, ov, lsem.at[4])
    l_m = local(mom, mv, lsem.at[5])

    l_c.wait()
    for j in range(1, T):
        got(ca.at[f, ty(-j)], ctr.at[j - 1], cts.at[j - 1], {"tensor": ty(-j)})

    def ag_send(s):
        if s < AGP:
            b = fz(-s)
            send(ca.at[b], ca.at[b], ags.at[0, s], agr.at[0, s], {"fsdp": fz(1)})
        if s < AGM:
            b = fz(s)
            send(ca.at[b], ca.at[b], ags.at[1, s], agr.at[1, s], {"fsdp": fz(-1)})

    def ag_step(s):
        if s <= AGP:
            got(ca.at[fz(-s)], agr.at[0, s - 1], ags.at[0, s - 1], {"fsdp": fz(-1)})
        if s <= AGM:
            got(ca.at[fz(s)], agr.at[1, s - 1], ags.at[1, s - 1], {"fsdp": fz(1)})
        ag_send(s)

    def dx_step(s):
        ks = [k for k, ok in ((-s, s <= AGP), (s, s <= AGM and s > 0)) if ok]
        bs = [fz(k) for k in ks]
        acc = None
        for q in range(T):
            lhs = jnp.concatenate([ca[b, q] for b in bs], axis=0) if len(bs) > 1 else ca[bs[0], q]
            p = lax.dot_general(lhs, wg[q], (((1,), (1,)), ((), ())), preferred_element_type=f32)
            acc = p if acc is None else acc + p
        for n, (k, b) in enumerate(zip(ks, bs)):
            r = acc[n * QR:(n + 1) * QR].astype(bf16)
            if k == 0:
                dx_o[:, pl.ds(pl.multiple_of(f * DB, DB), DB)] = r
            else:
                i = k % F - 1
                dxs[b] = r
                send(dxs.at[b], dx_blk(f), dxsm.at[i], dxr.at[i], {"fsdp": b})

    def y_step(s):
        for h in range(2):
            for d, hops, sgn in ((0, YP[h], 1), (1, YM[h], -1)):
                if s < hops:
                    got(yrr.at[d, h, s - 1], yrrs.at[d, h, s - 1], yrs.at[d, h, s - 1], yd(-sgn))
                    b = yy(sgn * (hops - s))
                    yss[d, h, s - 1] = (yrr[d, h, s - 1].astype(f32) + fr[b, h].astype(f32)).astype(bf16)
                    send(yss.at[d, h, s - 1], yrr.at[d, h, s], yrs.at[d, h, s], yrrs.at[d, h, s], yd(sgn))

    def y_last():
        for h in range(2):
            got(yrr.at[0, h, YP[h] - 1], yrrs.at[0, h, YP[h] - 1], yrs.at[0, h, YP[h] - 1], yd(-1))
            got(yrr.at[1, h, YM[h] - 1], yrrs.at[1, h, YM[h] - 1], yrs.at[1, h, YM[h] - 1], yd(1))
            ys[h] = (yrr[0, h, YP[h] - 1].astype(f32) + yrr[1, h, YM[h] - 1].astype(f32)
                     + fr[y, h].astype(f32)).astype(bf16)
            send(ys.at[h], xr.at[h], xss.at[h], xsr.at[h], xpart)

    def update(b, h):
        avg = ov[b, h] - sm[b, h].astype(f32) * (1.0 / (2 * Y))
        nm = beta_outer * mv[b, h] + avg
        nm_o[b, h] = nm
        no_o[b, h] = ov[b, h] - outer_rate * (avg + beta_outer * nm)

    def ya_send(s):
        for h in range(2):
            if s < YP[h]:
                b = yy(-s)
                send(sm.at[b, h], sm.at[b, h], yas.at[0, h, s], yar.at[0, h, s], yd(1))
            if s < YM[h]:
                b = yy(s)
                send(sm.at[b, h], sm.at[b, h], yas.at[1, h, s], yar.at[1, h, s], yd(-1))

    def ya_first():
        for h in range(2):
            got(xr.at[h], xsr.at[h], xss.at[h], xpart)
            sm[y, h] = (ys[h].astype(f32) + xr[h].astype(f32)).astype(bf16)
        ya_send(0)

    def upd(s):
        for h in range(2):
            if s <= YP[h]:
                update(yy(-s), h)
            if 0 < s <= YM[h]:
                update(yy(s), h)

    def ya_step(s):
        for h in range(2):
            if s <= YP[h]:
                b = yy(-s)
                got(sm.at[b, h], yar.at[0, h, s - 1], yas.at[0, h, s - 1], yd(-1))
            if s <= YM[h]:
                b = yy(s)
                got(sm.at[b, h], yar.at[1, h, s - 1], yas.at[1, h, s - 1], yd(1))
        ya_send(s)

    def k_make(s):
        ks = [k for k, ok in ((RSP - s, s <= RSP), (s - RSM, s < RSM)) if ok]
        for k in ks:
            if k == 0:
                l_x.wait()
            else:
                i = (-k) % F - 1
                got(xa.at[fz(k)], tkr.at[i], tks.at[i], {"fsdp": fz(k)})
        bs = [fz(k) for k in ks]
        lhs = jnp.concatenate([xa[b] for b in bs], axis=0) if len(bs) > 1 else xa[bs[0]]
        for q in range(T):
            r = jnp.dot(lhs, wg[q], preferred_element_type=f32)
            for n, b in enumerate(bs):
                kp[q, b] = r[n * QR:(n + 1) * QR]

    def k_step(s):
        for d, hops, sgn, rv, sd in ((0, RSP, 1, krp, ksp), (1, RSM, -1, krm, ksm)):
            if s < hops:
                b = fz(sgn * (hops - s))
                v = kp[:, b]
                if s > 0:
                    got(rv.at[s - 1], ksr.at[d, s - 1], kss.at[d, s - 1], {"fsdp": fz(-sgn)})
                    v = v + rv[s - 1].astype(f32)
                sd[s] = v.astype(bf16)
                send(sd.at[s], rv.at[s], kss.at[d, s], ksr.at[d, s], {"fsdp": fz(sgn)})

    def k_last():
        got(krp.at[RSP - 1], ksr.at[0, RSP - 1], kss.at[0, RSP - 1], {"fsdp": fz(-1)})
        got(krm.at[RSM - 1], ksr.at[1, RSM - 1], kss.at[1, RSM - 1], {"fsdp": fz(1)})
        kfin[...] = (kp[:, f] + krp[RSP - 1].astype(f32) + krm[RSM - 1].astype(f32)).astype(bf16)
        rows = pl.ds(pl.multiple_of(t * QR, QR), QR)
        mine = keys_o.at[rows, :]
        for j in range(1, T):
            q = ty(j)
            send(kfin.at[q], mine, kts.at[j - 1], ktr.at[j - 1], {"tensor": q})
        keys_o[rows, :] = kfin[t]

    far = 1 - xlo

    def w_one(q):
        r = lax.dot_general(xa[...].reshape(F * QR, DB), ca[:, q].reshape(F * QR, KT),
                            (((0,), (0,)), ((), ())), preferred_element_type=f32)
        dwp[q] = r.astype(bf16)

    def w_pair(m, i):
        w_one(2 * m + 1 - core)
        send(dwp.at[2 * m + 1 - core], dwr.at[i], dwss.at[i], dwsr.at[i], {"tensor": tc})
        w_one(2 * m + core)

    def w_mid():
        got(dwr.at[0], dwsr.at[0], dwss.at[0], {"tensor": tc})
        dws[...] = (dwp[2 * far + core].astype(f32) + dwr[0].astype(f32)).astype(bf16)
        send(dws, dwx, dwss.at[2], dwsr.at[2], {"tensor": tx})

    def w_last():
        got(dwr.at[1], dwsr.at[1], dwss.at[1], {"tensor": tc})
        got(dwx, dwsr.at[2], dwss.at[2], {"tensor": tx})
        dw_o[...] = (dwp[2 * xlo + core].astype(f32) + dwr[1].astype(f32) + dwx[...].astype(f32)).astype(bf16)

    ag_send(0)
    tok_send((4, -4, 3, -3))
    l_f.wait()
    y_step(1)
    ag_step(1)
    tok_send((2, -2, 1, -1))
    y_step(2)
    ag_step(2)
    got(wg.at[tx], wsr.at[0], wss.at[0], {"tensor": tx})
    send(wg.at[tx], wg.at[tx], wss.at[2], wsr.at[2], {"tensor": tc})
    l_w.wait()
    got(wg.at[tc], wsr.at[1], wss.at[1], {"tensor": tc})
    txc = lax.rem(tc + 2, T)
    got(wg.at[txc], wsr.at[2], wss.at[2], {"tensor": tc})
    k_make(0)
    k_step(0)
    dx_step(1)
    k_make(1)
    y_step(3)
    ag_step(3)
    k_step(1)
    dx_step(2)
    k_make(2)
    y_last()
    ag_step(4)
    k_step(2)
    dx_step(3)
    k_make(3)
    ya_first()
    ag_step(5)
    k_step(3)
    dx_step(4)
    k_make(4)
    ya_step(1)
    ag_step(6)
    k_step(4)
    dx_step(6)
    dx_step(5)
    k_make(5)
    w_pair(far, 0)
    ya_step(2)
    k_step(5)
    w_mid()
    ya_step(3)
    w_pair(xlo, 1)
    dx_step(0)
    k_last()
    l_o.wait()
    l_m.wait()
    for s in range(4):
        upd(s)
    ya_step(4)
    upd(4)
    w_last()
    for k in range(1, F):
        got(dx_blk(fz(-k)), dxr.at[k - 1], dxsm.at[k - 1], {"fsdp": fz(-k)})
    for j in range(1, T):
        q = ty(-j)
        got(keys_o.at[pl.ds(pl.multiple_of(q * QR, QR), QR), :], ktr.at[j - 1], kts.at[j - 1], {"tensor": q})
    for c in pending:
        c.wait_send()


def flush(*refs):
    n = len(refs) // 2
    sem = refs[-1]
    copies = [pltpu.make_async_copy(refs[i], refs[n + i], sem.at[i]) for i in (3, 4, 1, 2, 0)]
    for c in copies:
        c.start()
    for c in copies:
        c.wait()


def body(tokens, key_weight, key_cotangent, local_frag, outer_frag, momentum):
    FS = (Y, 2, 64, 512)
    V, DMA = pltpu.VMEM, pltpu.SemaphoreType.DMA
    blk = (T, QR, KT)
    hbm = pl.BlockSpec(memory_space=pltpu.HBM)
    vmem = pl.BlockSpec(memory_space=pltpu.VMEM)
    outs = (
        jax.ShapeDtypeStruct((T * QR, KT), bf16),
        jax.ShapeDtypeStruct((QR, F * DB), bf16),
        jax.ShapeDtypeStruct((DB, KT), bf16),
        jax.ShapeDtypeStruct(FS, f32),
        jax.ShapeDtypeStruct(FS, f32),
    )
    fixed = lambda a: pltpu.with_memory_space_constraint(a, pltpu.HBM)
    made = pl.pallas_call(
        kernel,
        out_shape=tuple(V(o.shape, o.dtype) for o in outs),
        in_specs=[hbm] * 6,
        out_specs=(vmem,) * 5,
        scratch_shapes=[
            V((F, QR, DB), bf16), V((F,) + blk, bf16), V((T, DB, KT), bf16), V((F, QR, DB), bf16),
            V((T, F, QR, KT), f32), V((RSP,) + blk, bf16), V((RSM,) + blk, bf16),
            V((RSP,) + blk, bf16), V((RSM,) + blk, bf16), V(blk, bf16),
            V((T, DB, KT), bf16), V((2, DB, KT), bf16), V((DB, KT), bf16), V((DB, KT), bf16),
            V(FS, bf16), V((2, 2, 3, 64, 512), bf16), V((2, 2, 4, 64, 512), bf16),
            V((2, 64, 512), bf16), V((2, 64, 512), bf16), V(FS, bf16),
            V(FS, f32), V(FS, f32),
            DMA((6,)), DMA((11,)), DMA((11,)), DMA((3,)), DMA((3,)), DMA((3,)), DMA((3,)),
            DMA((2, 6)), DMA((2, 6)), DMA((11,)), DMA((11,)), DMA((2, 6)), DMA((2, 6)), DMA((3,)), DMA((3,)),
            DMA((3,)), DMA((3,)), DMA((2, 2, 4)), DMA((2, 2, 4)), DMA((2,)), DMA((2,)),
            DMA((2, 2, 4)), DMA((2, 2, 4)),
        ],
        compiler_params=pltpu.CompilerParams(collective_id=0, has_side_effects=True,
                                             vmem_limit_bytes=40 << 20),
    )(*map(fixed, (tokens, key_weight[0], key_cotangent, local_frag.reshape(FS), outer_frag.reshape(FS), momentum.reshape(FS))))
    keys, dx, dw, no, nm = pl.pallas_call(
        flush,
        out_shape=outs,
        in_specs=[vmem] * 5,
        out_specs=(hbm,) * 5,
        scratch_shapes=[DMA((5,))],
        compiler_params=pltpu.CompilerParams(vmem_limit_bytes=1 << 20),
    )(*made)
    return keys, dx, dw[None], no.reshape(outer_frag.shape), nm.reshape(momentum.shape)


def solution(mesh):
    return jax.shard_map(
        body,
        mesh=mesh,
        in_specs=(
            P(("island", "fsdp"), None),
            P("island", "fsdp", "tensor"),
            P(("island", "fsdp"), "tensor"),
            P("island", None, "fsdp", "tensor"),
            P(None, "fsdp", "tensor"),
            P(None, "fsdp", "tensor"),
        ),
        out_specs=(
            P(("island", "fsdp"), "tensor"),
            P(("island", "fsdp", "tensor"), None),
            P("island", "fsdp", "tensor"),
            P(None, "fsdp", "tensor"),
            P(None, "fsdp", "tensor"),
        ),
        check_vma=False,
    )
```
